32 devices in a mesh: groups: 2 (over y), expert: 4 (over z), section: 4 (over x, core).
Axes of the slice: x: 2, y: 2, z: 4, core: 2. Of those that a mesh axis runs over, the one named last changes fastest.
Arguments:
- pending_microgroups: bfloat16 [4, 1024, 768], P('section', ('groups', 'expert')), parts along dimension 1, may hold values from -6 to 6
- arriving_microgroups: bfloat16 [2, 1024, 768], P(None, ('groups', 'expert')), parts along dimension 1, may hold values from -6 to 6
- expert_choice_grid: int32 [3, 4, 1024], P(None, 'section', ('groups', 'expert')), parts along dimension 2, may hold values from 0 to 1, as said below
- rootmean_gain: float32 [4, 768], P('section'), may hold values from 0.5 to 1.5
- gating_columns: bfloat16 [4, 768, 2], P('section'), may hold values from -0.21875 to 0.21875
- up_projection_matrix: bfloat16 [4, 4, 768, 768], P('section', 'expert'), may hold values from -0.21875 to 0.21875
- down_projection_matrix: bfloat16 [4, 4, 768, 768], P('section', 'expert'), may hold values from -0.21875 to 0.21875
Outputs:
- section_out: bfloat16 [4, 3, 1024, 768], P('section', None, ('groups', 'expert')), parts along dimension 2
The draws below stay inside these ranges and needn't reach their ends.
There are 2 independent parts, one for each index of `groups`. The reference program is written for one: setup_inputs(seed, part) draws one part's arguments, and reference() takes and returns one part's arrays. A program takes and returns all parts, laid end to end along the dimension named above; an argument that names none is the same for every part. Nothing has to cross between parts.
Inputs may be any that keep to these rules, and one draw needn't show every extreme that they name: `expert_choice_grid`: for every tick and section, no expert is named by more than 128 tokens of one aligned block of 128 tokens (the tokens of one device), and one expert, drawn from the seed, is named by exactly 128 tokens of every such block.
All inputs are finite; a program needn't handle non-finite values.
Results may differ from the reference program's by a relative error of at most 0.0095.
Values may be sent and summed in bfloat16 or wider, within the bound.
No kernel may reach another device: no remote copies, remote signals or barrier semaphores. Data moves between devices by JAX's collectives and lax.ppermute only.
A program may use at most 64 MiB of HBM per device.

```python
import jax
import jax.numpy as jnp
from jax import lax

EMBED_DIMENSION = 768
TICKS = 3
ROWS_DEV = 128
HID = 768
EXPERTS = 2
LEG_TOTAL = 4
MICRO_GROUP_SIZE = 512
CAP = 128
N_EXPERT = 4


def draw_expert_choice_grid(key, part):
    key = jax.random.fold_in(key, 11)
    blocks = MICRO_GROUP_SIZE // ROWS_DEV
    remain = ROWS_DEV - CAP
    others = max(EXPERTS - 1, 1)
    per_label = -(-remain // others)
    keep_limit = CAP - per_label
    position = jnp.arange(ROWS_DEV, dtype=jnp.int32)

    def one_block(block_key, hot_expert):
        key_pick, key_perm = jax.random.split(block_key)
        picked = jax.random.randint(key_pick, (ROWS_DEV,), 0, others, dtype=jnp.int32)
        in_rest = (position >= CAP).astype(jnp.int32)
        one_hot = (picked[:, None] == jnp.arange(others, dtype=jnp.int32)[None, :]).astype(jnp.int32) * in_rest[:, None]
        label_rank = jnp.sum((jnp.cumsum(one_hot, axis=0) - one_hot) * one_hot, axis=1)
        cyclic = (position - CAP) % others
        labels = jnp.where(label_rank < keep_limit, picked, cyclic)
        other_expert = labels + (labels >= hot_expert).astype(jnp.int32)
        chosen = jnp.where(position < CAP, hot_expert, other_expert)
        return chosen[jax.random.permutation(key_perm, ROWS_DEV)]

    def one_group(group_key):
        hot_key, rest_key = jax.random.split(group_key)
        hot_expert = jax.random.randint(hot_key, (), 0, EXPERTS, dtype=jnp.int32)
        block_keys = jax.random.split(rest_key, blocks)
        return jax.vmap(one_block, in_axes=(0, None))(block_keys, hot_expert).reshape(MICRO_GROUP_SIZE)
    group_keys = jax.random.split(key, TICKS * LEG_TOTAL)
    return jax.vmap(one_group)(group_keys).reshape(TICKS, LEG_TOTAL, MICRO_GROUP_SIZE).astype(jnp.int32)


def steps_of(rng, dims, cuts, smallest, high):
    gain, own = 1.0, jax.random.fold_in(rng, 6)
    for dim, blocks in cuts:
        draws = jnp.exp(jax.random.uniform(jax.random.fold_in(own, dim), (blocks,), jnp.float32, smallest / len(cuts), high / len(cuts)))
        gain = gain * jnp.repeat(draws, dims[dim] // blocks).reshape([-1 if axis == dim else 1 for axis in range(len(dims))])
    return gain


def normal_values(stream_key, dims, width, bound, cuts=(), kind=jnp.bfloat16):
    loudness = steps_of(stream_key, dims, cuts, -0.22, 0.18) if cuts else 1.0
    values = jax.random.normal(stream_key, dims, jnp.float32) * width * loudness
    return jnp.minimum(jnp.maximum(values, -bound), bound).astype(kind)


def setup_inputs(seed: int = 0, part: int = 0) -> dict:
    seeds = jax.random.split(jax.random.key(seed), 8)
    own_keys = jax.random.split(jax.random.fold_in(seeds[7], part), 8)
    pending_microgroups = normal_values(own_keys[0], (LEG_TOTAL, MICRO_GROUP_SIZE, EMBED_DIMENSION), 1.0, 6.0, ((0, 4), (1, 4)))
    arriving_microgroups = normal_values(own_keys[1], (TICKS - 1, MICRO_GROUP_SIZE, EMBED_DIMENSION), 1.0, 6.0, ((1, 4),))
    expert_choice_grid = draw_expert_choice_grid(jax.random.fold_in(jax.random.fold_in(seeds[7], part), 71), part)
    rootmean_gain = jnp.clip(1.0 + 0.1 * jax.random.normal(seeds[3], (LEG_TOTAL, EMBED_DIMENSION), jnp.float32), 0.5, 1.5)
    gating_columns = normal_values(seeds[4], (LEG_TOTAL, EMBED_DIMENSION, EXPERTS), EMBED_DIMENSION ** -0.5, 0.21875, ((0, 4),))
    up_projection_matrix = normal_values(seeds[5], (LEG_TOTAL, 2 * EXPERTS, EMBED_DIMENSION, HID), EMBED_DIMENSION ** -0.5, 0.21875, ((0, 4), (1, 4)))
    down_projection_matrix = normal_values(seeds[6], (LEG_TOTAL, 2 * EXPERTS, HID, EMBED_DIMENSION), HID ** -0.5, 0.21875, ((0, 4), (1, 4)))
    return dict(pending_microgroups=pending_microgroups, arriving_microgroups=arriving_microgroups, expert_choice_grid=expert_choice_grid, rootmean_gain=rootmean_gain, gating_columns=gating_columns, up_projection_matrix=up_projection_matrix, down_projection_matrix=down_projection_matrix)


def expert_layer(tok_rows, routes, rootmean_gain, gating_columns, up_projection_matrix, down_projection_matrix):
    float_rows = tok_rows.astype(jnp.float32)
    inv_rms = lax.rsqrt(lax.optimization_barrier(jnp.mean(float_rows * float_rows, axis=-1, keepdims=True)) + 1e-06)
    normed = (float_rows * inv_rms * rootmean_gain.astype(jnp.float32)).astype(jnp.bfloat16)
    logits = jnp.dot(normed, gating_columns, preferred_element_type=jnp.float32)
    gate_value = jax.nn.sigmoid(jnp.take_along_axis(logits, routes[:, None].astype(jnp.int32), axis=1)[:, 0])
    row_limit = N_EXPERT * CAP

    def per_expert(expert):
        chosen = routes == expert
        row_index = jnp.nonzero(chosen, size=row_limit, fill_value=0)[0].astype(jnp.int32)
        is_valid = jnp.arange(row_limit, dtype=jnp.int32) < jnp.sum(chosen.astype(jnp.int32))
        picked = normed[row_index]
        partials = []
        for half_idx in range(2):
            hidden = jnp.maximum(jnp.dot(picked, up_projection_matrix[2 * expert + half_idx], preferred_element_type=jnp.float32), 0.0).astype(jnp.bfloat16)
            partials.append(jnp.dot(hidden, down_projection_matrix[2 * expert + half_idx], preferred_element_type=jnp.float32).astype(jnp.bfloat16))
        merged = (partials[0].astype(jnp.float32) + partials[1].astype(jnp.float32)).astype(jnp.bfloat16)
        merged = lax.optimization_barrier(merged)
        return (row_index, jnp.where(is_valid[:, None], merged.astype(jnp.float32), jnp.float32(0.0)))
    row_index, values = lax.map(per_expert, jnp.arange(EXPERTS, dtype=jnp.int32))
    expert_out = jnp.zeros(float_rows.shape, jnp.float32).at[row_index.reshape(-1)].add(values.reshape(-1, EMBED_DIMENSION))
    return (float_rows + gate_value[:, None] * expert_out).astype(jnp.bfloat16)

def reference(pending_microgroups, arriving_microgroups, expert_choice_grid, rootmean_gain, gating_columns, up_projection_matrix, down_projection_matrix):
    running_activation = [pending_microgroups[leg_position] for leg_position in range(LEG_TOTAL)]
    per_tick = []
    for tick_idx in range(TICKS):
        outputs = [expert_layer(running_activation[leg_position], expert_choice_grid[tick_idx, leg_position], rootmean_gain[leg_position], gating_columns[leg_position], up_projection_matrix[leg_position], down_projection_matrix[leg_position]) for leg_position in range(LEG_TOTAL)]
        per_tick.append(jnp.stack(outputs))
        if tick_idx + 1 < TICKS:
            running_activation = [arriving_microgroups[tick_idx]] + outputs[:-1]
    return jnp.stack(per_tick, axis=1)
```

```python
import functools

import jax
import jax.numpy as jnp
from jax import lax
from jax.experimental import pallas as pl
from jax.experimental.pallas import tpu as pltpu
from jax.sharding import PartitionSpec as P

TICKS = 3


def swapped(x, axis, bit):
    return lax.ppermute(x, axis, [(i, i ^ 1 << bit) for i in range(lax.axis_size(axis))])


def from_behind(value, axis, steps):
    count = lax.axis_size(axis)
    initial, last = (max(0, -steps), min(count, count - steps))
    return lax.ppermute(value, axis, [(source, source + steps) for source in range(initial, last)])


def half_output(received, up_projection_matrix, down_projection_matrix):
    hidden = jnp.maximum(
        jnp.einsum(
            "sid,dh->sih", received, up_projection_matrix, preferred_element_type=jnp.float32
        ),
        0.0,
    ).astype(jnp.bfloat16)
    return jnp.einsum(
        "sih,hd->sid", hidden, down_projection_matrix, preferred_element_type=jnp.float32
    ).astype(jnp.bfloat16)


def expert_layer(
    tok_rows,
    routes,
    rootmean_gain,
    gating_columns,
    up_projection_matrix,
    down_projection_matrix,
    other_in,
    other_out,
):
    num_rows, width = tok_rows.shape
    experts = gating_columns.shape[1]
    capacity = min(num_rows, 3 * num_rows // experts)
    float_rows = tok_rows.astype(jnp.float32)
    inv_rms = lax.rsqrt(jnp.mean(float_rows * float_rows, axis=-1, keepdims=True) + 1e-06)
    normed = (float_rows * inv_rms * rootmean_gain).astype(jnp.bfloat16)
    logits = jnp.dot(normed, gating_columns, preferred_element_type=jnp.float32)
    one_hot = routes[:, None] == jnp.arange(experts, dtype=jnp.int32)[None, :]
    gate_value = jax.nn.sigmoid(jnp.sum(jnp.where(one_hot, logits, 0.0), axis=1))
    flags = one_hot.astype(jnp.int32)
    slot_rank = jnp.sum((jnp.cumsum(flags, axis=0) - flags) * flags, axis=1)
    slot_index = routes * capacity + slot_rank
    placing = (
        slot_index[None, :] == jnp.arange(experts * capacity, dtype=jnp.int32)[:, None]
    ).astype(jnp.bfloat16)
    outgoing = jnp.dot(placing, normed, preferred_element_type=jnp.float32).astype(jnp.bfloat16)
    outgoing = outgoing.reshape(experts, capacity, width)
    halves = outgoing.reshape(2 * experts, capacity // 2, width)
    received = lax.all_to_all(halves, "expert", split_axis=0, concat_axis=0, tiled=True)
    own_part = half_output(received, up_projection_matrix, down_projection_matrix)
    other_part = half_output(received, other_in, other_out)
    summed = (own_part.astype(jnp.float32) + other_part.astype(jnp.float32)).astype(jnp.bfloat16)
    combined = lax.all_to_all(summed, "expert", split_axis=0, concat_axis=0, tiled=True)
    flat_out = combined.reshape(experts * capacity, width)
    expert_out = lax.dot_general(
        placing, flat_out, (((0,), (0,)), ((), ())), preferred_element_type=jnp.float32
    )
    return (float_rows + gate_value[:, None] * expert_out).astype(jnp.bfloat16)


def slots_per_device(
    pending_microgroups,
    arriving_microgroups,
    expert_choice_grid,
    rootmean_gain,
    gating_columns,
    up_projection_matrix,
    down_projection_matrix,
):
    leg_position = lax.axis_index("section")
    own_in = up_projection_matrix[0, 0]
    own_out = down_projection_matrix[0, 0]
    other_in, other_out = swapped((own_in, own_out), "expert", 0)
    running_activation = pending_microgroups[0]
    per_tick = []
    for tick_idx in range(TICKS):
        layer_out = expert_layer(
            running_activation,
            expert_choice_grid[tick_idx, 0],
            rootmean_gain[0],
            gating_columns[0],
            own_in,
            own_out,
            other_in,
            other_out,
        )
        per_tick.append(layer_out)
        if tick_idx + 1 < TICKS:
            moved = from_behind(layer_out, "section", 1)
            running_activation = jnp.where(leg_position == 0, arriving_microgroups[tick_idx], moved)
    return jnp.stack(per_tick)[None]


def piece_list(width, splits):
    share = width // splits
    size = share // 3 if share % 3 == 0 and (share // 3) % 128 == 0 else share
    return [(m, r, size) for m in (0, 1) for r in range(0, share, size)]


def layer_kernel(pieces, share, splits, summing, *refs):
    refs = list(refs)
    take = refs.pop
    flags_ref = take(0)
    if summing:
        straight_ref, cross_ref, fresh_ref = take(0), take(0), take(0)
    else:
        rows_ref = take(0)
    keep_ref, gain_ref, column_ref = take(0), take(0), take(0)
    own_refs = [take(0), take(0)]
    near_refs = [take(0) for _ in pieces]
    far_refs = [take(0) for _ in pieces]
    y_ref = take(0)
    moved_ref = take(0) if summing else None
    own_w, other_w, sems = refs

    group = flags_ref[0]
    copies = [[], []]
    index = 0
    for m in (0, 1):
        copies[m].append(pltpu.make_async_copy(own_refs[m], own_w.at[m], sems.at[index]))
        index += 1
        for (pm, first, size), near, far in zip(pieces, near_refs, far_refs):
            if pm != m:
                continue
            for ref, part in ((near, group), (far, splits - 1 - group)):
                start = pl.multiple_of(part * share + first, 128)
                copies[m].append(
                    pltpu.make_async_copy(
                        ref, other_w.at[m, pl.ds(start, size), :], sems.at[index]
                    )
                )
                index += 1
    for copy in copies[0] + copies[1]:
        copy.start()

    if summing:
        moved = straight_ref[...].astype(jnp.float32) + cross_ref[...].astype(jnp.float32)
        moved_ref[...] = moved.astype(jnp.bfloat16)
        x = jnp.where(flags_ref[1] == 0, fresh_ref[...].astype(jnp.float32), moved)
    else:
        x = rows_ref[...].astype(jnp.float32)
    inv_rms = lax.rsqrt(jnp.mean(x * x, axis=-1, keepdims=True) + 1e-06)
    normed = (x * inv_rms * gain_ref[...]).astype(jnp.bfloat16)
    logit = jnp.sum(normed.astype(jnp.float32) * column_ref[...], axis=-1, keepdims=True)
    gate = jax.nn.sigmoid(logit)
    hidden = []
    for copy in copies[0]:
        copy.wait()
    for w in (own_w, other_w):
        up = jnp.dot(normed, w[0], preferred_element_type=jnp.float32)
        hidden.append(jnp.maximum(up, 0.0).astype(jnp.bfloat16))
    for copy in copies[1]:
        copy.wait()
    out = jnp.dot(hidden[0], own_w[1], preferred_element_type=jnp.float32)
    out = out + jnp.dot(hidden[1], other_w[1], preferred_element_type=jnp.float32)
    y = x + gate * out
    y_ref[...] = jnp.where(keep_ref[...] != 0, y, 0.0).astype(jnp.bfloat16)


def pairs_per_device(
    pending_microgroups,
    arriving_microgroups,
    expert_choice_grid,
    rootmean_gain,
    gating_columns,
    up_projection_matrix,
    down_projection_matrix,
):
    group = lax.axis_index("groups")
    leg = lax.axis_index("section")
    place = lax.axis_index("expert")
    splits = lax.axis_size("groups")
    places = lax.axis_size("expert")
    legs = lax.axis_size("section")
    side = place // 2
    own = (up_projection_matrix[0, 0], down_projection_matrix[0, 0])
    width, hid = own[0].shape
    num_rows = pending_microgroups.shape[1]
    share = width // splits
    pieces = piece_list(width, splits)

    near = []
    for m, first, size in pieces:
        piece = lax.dynamic_slice(own[m], (group * share + first, 0), (size, hid))
        near.append(swapped(piece, "expert", 0))
    far = [swapped(piece, "groups", 0) for piece in near]

    flags = jnp.stack([group, leg]).astype(jnp.int32)
    gain = rootmean_gain[:1]
    column = lax.dynamic_slice(gating_columns[0], (0, side), (width, 1))
    column = column.astype(jnp.float32).reshape(1, width)
    routes = expert_choice_grid[:, 0]
    keep_own = (routes == side).astype(jnp.int32)[:, :, None]
    keep_other = (swapped(routes, "expert", 1) == side).astype(jnp.int32)[:, :, None]
    keeps = (keep_own, keep_other)

    own_rows = pending_microgroups[0]
    other_rows = swapped(own_rows, "expert", 1)
    pairs = [(e * legs, (e ^ 2) * legs) for e in range(places)]
    fresh_other = lax.ppermute(arriving_microgroups, ("expert", "section"), pairs)
    fresh = (arriving_microgroups, fresh_other)

    def layer(tick, which, parts):
        summing = len(parts) == 2
        operands = [flags]
        operands += [*parts, fresh[which][tick - 1]] if summing else list(parts)
        operands += [keeps[which][tick], gain, column]
        in_vmem = pl.BlockSpec(memory_space=pltpu.VMEM)
        in_specs = [pl.BlockSpec(memory_space=pltpu.SMEM)] + [in_vmem] * (len(operands) - 1)
        weights = [*own, *near, *far]
        in_specs += [pl.BlockSpec(memory_space=pl.ANY)] * len(weights)
        rows_shape = jax.ShapeDtypeStruct((num_rows, width), jnp.bfloat16)
        outs = [rows_shape] * (2 if summing else 1)
        return pl.pallas_call(
            functools.partial(layer_kernel, pieces, share, splits, summing),
            out_shape=outs,
            in_specs=in_specs,
            out_specs=[in_vmem] * len(outs),
            scratch_shapes=[
                pltpu.VMEM((2, width, hid), jnp.bfloat16),
                pltpu.VMEM((2, width, hid), jnp.bfloat16),
                pltpu.SemaphoreType.DMA((len(weights),)),
            ],
            compiler_params=pltpu.CompilerParams(vmem_limit_bytes=24 << 20),
            name=f"layer_{tick}_{which}",
        )(*operands, *weights)

    def ahead(value, flip, wrap):
        last = legs if wrap else legs - 1
        perm = [
            (e * legs + s, (e ^ flip) * legs + (s + 1) % legs)
            for e in range(places)
            for s in range(last)
        ]
        return lax.ppermute(value, ("expert", "section"), perm)

    def back(value):
        return lax.ppermute(value, "section", [((s + 1) % legs, s) for s in range(legs)])

    current = {0: (own_rows,), 1: (other_rows,)}
    outputs = []
    for tick in range(TICKS):
        order = (1, 0) if tick % 2 == 0 else (0, 1)
        following = {}
        done = {}
        for which in order:
            got = layer(tick, which, current[which])
            done[which] = got[0]
            if len(got) == 2 and which == 0:
                outputs.append(back(got[1]))
            if tick + 1 < TICKS:
                arrives = 1 - which
                following[arrives] = ahead(got[0], 2, arrives == 0)
            elif which == 1:
                returned = swapped(got[0], "expert", 1)
        if tick + 1 < TICKS:
            current = {w: (ahead(done[w], 0, w == 0), following[w]) for w in (0, 1)}
    outputs.append((done[0] + returned).astype(jnp.bfloat16))
    return jnp.stack(outputs)[None]


def solution(mesh):
    placed = (
        P("section", ("groups", "expert"), None),
        P(None, ("groups", "expert"), None),
        P(None, "section", ("groups", "expert")),
        P("section", None),
        P("section", None, None),
        P("section", "expert", None, None),
        P("section", "expert", None, None),
    )

    def per_device(*args):
        experts = args[4].shape[2]
        if experts == 2 and mesh.shape["expert"] == 4 and mesh.shape["groups"] == 2:
            return pairs_per_device(*args)
        return slots_per_device(*args)

    return jax.shard_map(
        per_device,
        mesh=mesh,
        in_specs=placed,
        out_specs=P("section", None, ("groups", "expert"), None),
        check_vma=False,
    )
```

```python
import functools

import jax
import jax.numpy as jnp
from jax import lax
from jax.experimental import pallas as pl
from jax.experimental.pallas import tpu as pltpu
from jax.sharding import PartitionSpec as P

TICKS = 3


def swapped(x, axis, bit):
    return lax.ppermute(x, axis, [(i, i ^ 1 << bit) for i in range(lax.axis_size(axis))])


def from_behind(value, axis, steps):
    count = lax.axis_size(axis)
    initial, last = (max(0, -steps), min(count, count - steps))
    return lax.ppermute(value, axis, [(source, source + steps) for source in range(initial, last)])


def half_output(received, up_projection_matrix, down_projection_matrix):
    hidden = jnp.maximum(
        jnp.einsum(
            "sid,dh->sih", received, up_projection_matrix, preferred_element_type=jnp.float32
        ),
        0.0,
    ).astype(jnp.bfloat16)
    return jnp.einsum(
        "sih,hd->sid", hidden, down_projection_matrix, preferred_element_type=jnp.float32
    ).astype(jnp.bfloat16)


def expert_layer(
    tok_rows,
    routes,
    rootmean_gain,
    gating_columns,
    up_projection_matrix,
    down_projection_matrix,
    other_in,
    other_out,
):
    num_rows, width = tok_rows.shape
    experts = gating_columns.shape[1]
    capacity = min(num_rows, 3 * num_rows // experts)
    float_rows = tok_rows.astype(jnp.float32)
    inv_rms = lax.rsqrt(jnp.mean(float_rows * float_rows, axis=-1, keepdims=True) + 1e-06)
    normed = (float_rows * inv_rms * rootmean_gain).astype(jnp.bfloat16)
    logits = jnp.dot(normed, gating_columns, preferred_element_type=jnp.float32)
    one_hot = routes[:, None] == jnp.arange(experts, dtype=jnp.int32)[None, :]
    gate_value = jax.nn.sigmoid(jnp.sum(jnp.where(one_hot, logits, 0.0), axis=1))
    flags = one_hot.astype(jnp.int32)
    slot_rank = jnp.sum((jnp.cumsum(flags, axis=0) - flags) * flags, axis=1)
    slot_index = routes * capacity + slot_rank
    placing = (
        slot_index[None, :] == jnp.arange(experts * capacity, dtype=jnp.int32)[:, None]
    ).astype(jnp.bfloat16)
    outgoing = jnp.dot(placing, normed, preferred_element_type=jnp.float32).astype(jnp.bfloat16)
    outgoing = outgoing.reshape(experts, capacity, width)
    halves = outgoing.reshape(2 * experts, capacity // 2, width)
    received = lax.all_to_all(halves, "expert", split_axis=0, concat_axis=0, tiled=True)
    own_part = half_output(received, up_projection_matrix, down_projection_matrix)
    other_part = half_output(received, other_in, other_out)
    summed = (own_part.astype(jnp.float32) + other_part.astype(jnp.float32)).astype(jnp.bfloat16)
    combined = lax.all_to_all(summed, "expert", split_axis=0, concat_axis=0, tiled=True)
    flat_out = combined.reshape(experts * capacity, width)
    expert_out = lax.dot_general(
        placing, flat_out, (((0,), (0,)), ((), ())), preferred_element_type=jnp.float32
    )
    return (float_rows + gate_value[:, None] * expert_out).astype(jnp.bfloat16)


def slots_per_device(
    pending_microgroups,
    arriving_microgroups,
    expert_choice_grid,
    rootmean_gain,
    gating_columns,
    up_projection_matrix,
    down_projection_matrix,
):
    leg_position = lax.axis_index("section")
    own_in = up_projection_matrix[0, 0]
    own_out = down_projection_matrix[0, 0]
    other_in, other_out = swapped((own_in, own_out), "expert", 0)
    running_activation = pending_microgroups[0]
    per_tick = []
    for tick_idx in range(TICKS):
        layer_out = expert_layer(
            running_activation,
            expert_choice_grid[tick_idx, 0],
            rootmean_gain[0],
            gating_columns[0],
            own_in,
            own_out,
            other_in,
            other_out,
        )
        per_tick.append(layer_out)
        if tick_idx + 1 < TICKS:
            moved = from_behind(layer_out, "section", 1)
            running_activation = jnp.where(leg_position == 0, arriving_microgroups[tick_idx], moved)
    return jnp.stack(per_tick)[None]


def piece_list(share):
    third = share // 3
    if third * 3 != share or third % 128:
        return [(m, 0, share) for m in (0, 1)]
    return [(0, 0, third), (0, third, 2 * third), (1, 0, 2 * third), (1, 2 * third, third)]


def in_pieces(rows, firsts, near_refs, far_refs, share, group):
    low, high = rows[:, :share], rows[:, share:]
    near_rows = jnp.where(group == 0, low, high)
    far_rows = jnp.where(group == 0, high, low)
    total = None
    for first, near, far in zip(firsts, near_refs, far_refs):
        size = near.shape[0]
        for part, ref in ((near_rows, near), (far_rows, far)):
            term = jnp.dot(
                part[:, first : first + size], ref[...], preferred_element_type=jnp.float32
            )
            total = term if total is None else total + term
    return total


def layer_kernel(tick, pieces, share, summing, moving, *refs):
    refs = list(refs)
    take = refs.pop
    routes_ref = take(0)
    parts = [take(0) for _ in range(3 if summing else 1)]
    gain_ref, columns_ref, up_ref, down_ref = take(0), take(0), take(0), take(0)
    near_refs = [take(0) for _ in pieces]
    far_refs = [take(0) for _ in pieces]
    take(0)
    y_ref = take(0)
    group = lax.axis_index("groups")
    side = lax.axis_index("expert") // 2
    if summing:
        straight_ref, cross_ref, fresh_ref = parts
        moved = straight_ref[...].astype(jnp.float32) + cross_ref[...].astype(jnp.float32)
        if moving:
            take(0)[...] = moved.astype(jnp.bfloat16)
        fresh = fresh_ref[tick - 1].astype(jnp.float32)
        x = jnp.where(lax.axis_index("section") == 0, fresh, moved)
    else:
        x = parts[0][...].astype(jnp.float32)
    inv_rms = lax.rsqrt(jnp.mean(x * x, axis=-1, keepdims=True) + 1e-06)
    normed = (x * inv_rms * gain_ref[...]).astype(jnp.bfloat16)
    columns = columns_ref[...].astype(jnp.float32)
    column = jnp.where(side == 0, columns[0:1], columns[1:2])
    logit = jnp.sum(normed.astype(jnp.float32) * column, axis=-1, keepdims=True)
    gate = jax.nn.sigmoid(logit)

    def pick(refs, m):
        return [ref for ref, piece in zip(refs, pieces) if piece[0] == m]

    firsts = [[first for pm, first, _ in pieces if pm == m] for m in (0, 1)]
    up = jnp.dot(normed, up_ref[...], preferred_element_type=jnp.float32)
    hidden = jnp.maximum(up, 0.0).astype(jnp.bfloat16)
    up = in_pieces(normed, firsts[0], pick(near_refs, 0), pick(far_refs, 0), share, group)
    other = jnp.maximum(up, 0.0).astype(jnp.bfloat16)
    out = jnp.dot(hidden, down_ref[...], preferred_element_type=jnp.float32)
    out = out + in_pieces(other, firsts[1], pick(near_refs, 1), pick(far_refs, 1), share, group)
    y = x + gate * out
    y_ref[...] = jnp.where(routes_ref[tick, 0, 0] == side, y, 0.0).astype(jnp.bfloat16)


def gather_kernel(first_ref, second_ref, own_ref, returned_ref, out_ref):
    out_ref[0, 0] = first_ref[...]
    out_ref[0, 1] = second_ref[...]
    total = own_ref[...].astype(jnp.float32) + returned_ref[...].astype(jnp.float32)
    out_ref[0, 2] = total.astype(jnp.bfloat16)


def pairs_per_device(
    pending_microgroups,
    arriving_microgroups,
    expert_choice_grid,
    rootmean_gain,
    gating_columns,
    up_projection_matrix,
    down_projection_matrix,
):
    group = lax.axis_index("groups")
    splits = lax.axis_size("groups")
    places = lax.axis_size("expert")
    legs = lax.axis_size("section")
    own = (up_projection_matrix[0, 0], down_projection_matrix[0, 0])
    width, hid = own[0].shape
    num_rows = pending_microgroups.shape[1]
    share = width // splits
    pieces = piece_list(share)

    near = []
    for m, first, size in pieces:
        source = own[m]
        if near:
            source, near[-1] = lax.optimization_barrier((source, near[-1]))
        near.append(lax.dynamic_slice(source, (group * share + first, 0), (size, hid)))
    near = [swapped(piece, "expert", 0) for piece in near]
    far = [swapped(piece, "groups", 0) for piece in near]

    columns = jnp.swapaxes(gating_columns[0], 0, 1)
    own_rows = pending_microgroups[0]
    other_rows = swapped(own_rows, "expert", 1)
    pairs = [(e * legs, (e ^ 2) * legs) for e in range(places)]
    fresh_other = lax.ppermute(arriving_microgroups, ("expert", "section"), pairs)
    fresh = (arriving_microgroups, fresh_other)
    in_vmem = pl.BlockSpec(memory_space=pltpu.VMEM)
    anywhere = pl.BlockSpec(memory_space=pl.ANY)
    rows_shape = jax.ShapeDtypeStruct((num_rows, width), jnp.bfloat16)

    def layer(tick, which, parts, after):
        summing = len(parts) == 2
        moving = summing and which == 0
        operands = [expert_choice_grid, *parts]
        if summing:
            operands.append(fresh[which])
        operands += [rootmean_gain, columns, *own, *near, *far]
        in_specs = [pl.BlockSpec(memory_space=pltpu.SMEM)] + [in_vmem] * (len(operands) - 1)
        outs = [rows_shape] * (2 if moving else 1)
        return pl.pallas_call(
            functools.partial(layer_kernel, tick, pieces, share, summing, moving),
            out_shape=outs,
            in_specs=[*in_specs, anywhere],
            out_specs=[in_vmem] * len(outs),
            compiler_params=pltpu.CompilerParams(vmem_limit_bytes=24 << 20),
            name=f"layer_{tick}_{which}",
        )(*operands, after)

    def ahead(value, flip, wrap):
        last = legs if wrap else legs - 1
        perm = [
            (e * legs + s, (e ^ flip) * legs + (s + 1) % legs)
            for e in range(places)
            for s in range(last)
        ]
        return lax.ppermute(value, ("expert", "section"), perm)

    def back(value):
        return lax.ppermute(value, "section", [((s + 1) % legs, s) for s in range(legs)])

    current = {0: (own_rows,), 1: (other_rows,)}
    outputs = []
    after = own_rows
    for tick in range(TICKS):
        order = (1, 0) if tick % 2 == 0 else (0, 1)
        following = {}
        straight = {}
        done = {}
        for which in order:
            got = layer(tick, which, current[which], after)
            after = done[which] = got[0]
            if tick + 1 < TICKS:
                arrives = 1 - which
                following[arrives] = ahead(got[0], 2, arrives == 0)
                straight[which] = ahead(got[0], 0, which == 0)
            elif which == 1:
                returned = swapped(got[0], "expert", 1)
            if len(got) == 2:
                outputs.append(back(got[1]))
        if tick + 1 < TICKS:
            current = {w: (straight[w], following[w]) for w in (0, 1)}
    return pl.pallas_call(
        gather_kernel,
        out_shape=jax.ShapeDtypeStruct((1, TICKS, num_rows, width), jnp.bfloat16),
        in_specs=[in_vmem] * 4,
        out_specs=in_vmem,
        name="gather",
    )(*outputs, done[0], returned)


def solution(mesh):
    placed = (
        P("section", ("groups", "expert"), None),
        P(None, ("groups", "expert"), None),
        P(None, "section", ("groups", "expert")),
        P("section", None),
        P("section", None, None),
        P("section", "expert", None, None),
        P("section", "expert", None, None),
    )

    def per_device(*args):
        experts = args[4].shape[2]
        if experts == 2 and mesh.shape["expert"] == 4 and mesh.shape["groups"] == 2:
            return pairs_per_device(*args)
        return slots_per_device(*args)

    return jax.shard_map(
        per_device,
        mesh=mesh,
        in_specs=placed,
        out_specs=P("section", None, ("groups", "expert"), None),
        check_vma=False,
    )
```

```python
import functools

import jax
import jax.numpy as jnp
from jax import lax
from jax.experimental import pallas as pl
from jax.experimental.pallas import tpu as pltpu
from jax.sharding import PartitionSpec as P


TICKS = 3


def swapped(x, axis, bit):
    return lax.ppermute(x, axis, [(i, i ^ 1 << bit) for i in range(lax.axis_size(axis))])


def from_behind(value, axis, steps):
    count = lax.axis_size(axis)
    initial, last = (max(0, -steps), min(count, count - steps))
    return lax.ppermute(value, axis, [(source, source + steps) for source in range(initial, last)])


def half_output(received, up_projection_matrix, down_projection_matrix):
    hidden = jnp.maximum(
        jnp.einsum(
            "sid,dh->sih", received, up_projection_matrix, preferred_element_type=jnp.float32
        ),
        0.0,
    ).astype(jnp.bfloat16)
    return jnp.einsum(
        "sih,hd->sid", hidden, down_projection_matrix, preferred_element_type=jnp.float32
    ).astype(jnp.bfloat16)


def expert_layer(
    tok_rows,
    routes,
    rootmean_gain,
    gating_columns,
    up_projection_matrix,
    down_projection_matrix,
    other_in,
    other_out,
):
    num_rows, width = tok_rows.shape
    experts = gating_columns.shape[1]
    capacity = min(num_rows, 3 * num_rows // experts)
    float_rows = tok_rows.astype(jnp.float32)
    inv_rms = lax.rsqrt(jnp.mean(float_rows * float_rows, axis=-1, keepdims=True) + 1e-06)
    normed = (float_rows * inv_rms * rootmean_gain).astype(jnp.bfloat16)
    logits = jnp.dot(normed, gating_columns, preferred_element_type=jnp.float32)
    one_hot = routes[:, None] == jnp.arange(experts, dtype=jnp.int32)[None, :]
    gate_value = jax.nn.sigmoid(jnp.sum(jnp.where(one_hot, logits, 0.0), axis=1))
    flags = one_hot.astype(jnp.int32)
    slot_rank = jnp.sum((jnp.cumsum(flags, axis=0) - flags) * flags, axis=1)
    slot_index = routes * capacity + slot_rank
    placing = (
        slot_index[None, :] == jnp.arange(experts * capacity, dtype=jnp.int32)[:, None]
    ).astype(jnp.bfloat16)
    outgoing = jnp.dot(placing, normed, preferred_element_type=jnp.float32).astype(jnp.bfloat16)
    outgoing = outgoing.reshape(experts, capacity, width)
    halves = outgoing.reshape(2 * experts, capacity // 2, width)
    received = lax.all_to_all(halves, "expert", split_axis=0, concat_axis=0, tiled=True)
    own_part = half_output(received, up_projection_matrix, down_projection_matrix)
    other_part = half_output(received, other_in, other_out)
    summed = (own_part.astype(jnp.float32) + other_part.astype(jnp.float32)).astype(jnp.bfloat16)
    combined = lax.all_to_all(summed, "expert", split_axis=0, concat_axis=0, tiled=True)
    flat_out = combined.reshape(experts * capacity, width)
    expert_out = lax.dot_general(
        placing, flat_out, (((0,), (0,)), ((), ())), preferred_element_type=jnp.float32
    )
    return (float_rows + gate_value[:, None] * expert_out).astype(jnp.bfloat16)


def slots_per_device(
    pending_microgroups,
    arriving_microgroups,
    expert_choice_grid,
    rootmean_gain,
    gating_columns,
    up_projection_matrix,
    down_projection_matrix,
):
    leg_position = lax.axis_index("section")
    own_in = up_projection_matrix[0, 0]
    own_out = down_projection_matrix[0, 0]
    other_in, other_out = swapped((own_in, own_out), "expert", 0)
    running_activation = pending_microgroups[0]
    per_tick = []
    for tick_idx in range(TICKS):
        layer_out = expert_layer(
            running_activation,
            expert_choice_grid[tick_idx, 0],
            rootmean_gain[0],
            gating_columns[0],
            own_in,
            own_out,
            other_in,
            other_out,
        )
        per_tick.append(layer_out)
        if tick_idx + 1 < TICKS:
            moved = from_behind(layer_out, "section", 1)
            running_activation = jnp.where(leg_position == 0, arriving_microgroups[tick_idx], moved)
    return jnp.stack(per_tick)[None]


def piece_list(share):
    third = share // 3
    if third * 3 != share or third % 128:
        return [(m, 0, share) for m in (0, 1)]
    return [(0, 0, third), (0, third, 2 * third), (1, 0, 2 * third), (1, 2 * third, third)]


def in_pieces(rows, firsts, near_refs, far_refs, share, group):
    low, high = rows[:, :share], rows[:, share:]
    near_rows = jnp.where(group == 0, low, high)
    far_rows = jnp.where(group == 0, high, low)
    total = None
    for first, near, far in zip(firsts, near_refs, far_refs):
        size = near.shape[0]
        for part, ref in ((near_rows, near), (far_rows, far)):
            term = jnp.dot(
                part[:, first : first + size], ref[...], preferred_element_type=jnp.float32
            )
            total = term if total is None else total + term
    return total


def cut_kernel(pieces, share, *refs):
    count = len(pieces)
    sources, outs, sems = refs[:-count - 1], refs[-count - 1 : -1], refs[-1]
    start = lax.axis_index("groups") * share
    copies = []
    for index, ((m, first, size), out) in enumerate(zip(pieces, outs)):
        rows = pl.ds(pl.multiple_of(start + first, 128), size)
        copies.append(pltpu.make_async_copy(sources[m].at[rows, :], out, sems.at[index]))
    for copy in copies:
        copy.start()
    for copy in copies:
        copy.wait()


def join_kernel(firsts, share, *refs):
    count = len(firsts)
    near_refs, far_refs, out_ref = refs[:count], refs[count : 2 * count], refs[-1]
    group = lax.axis_index("groups")
    for first, near, far in zip(firsts, near_refs, far_refs):
        size = near.shape[0]
        for part, ref in ((group, near), (1 - group, far)):
            out_ref[pl.ds(pl.multiple_of(part * share + first, 128), size), :] = ref[...]


def layer_kernel(tick, firsts, share, summing, moving, *refs):
    refs = list(refs)
    take = refs.pop
    routes_ref = take(0)
    parts = [take(0) for _ in range(3 if summing else 1)]
    gain_ref, columns_ref, up_ref, down_ref, far_up_ref = [take(0) for _ in range(5)]
    far_down_refs = [take(0) for _ in range(1 if summing else 2 * len(firsts))]
    take(0)
    y_ref = take(0)
    side = lax.axis_index("expert") // 2
    if summing:
        straight_ref, cross_ref, fresh_ref = parts
        moved = straight_ref[...].astype(jnp.float32) + cross_ref[...].astype(jnp.float32)
        if moving:
            take(0)[...] = moved.astype(jnp.bfloat16)
        fresh = fresh_ref[tick - 1].astype(jnp.float32)
        x = jnp.where(lax.axis_index("section") == 0, fresh, moved)
    else:
        x = parts[0][...].astype(jnp.float32)
    inv_rms = lax.rsqrt(jnp.mean(x * x, axis=-1, keepdims=True) + 1e-06)
    normed = (x * inv_rms * gain_ref[...]).astype(jnp.bfloat16)
    columns = columns_ref[...].astype(jnp.float32)
    column = jnp.where(side == 0, columns[0:1], columns[1:2])
    logit = jnp.sum(normed.astype(jnp.float32) * column, axis=-1, keepdims=True)
    gate = jax.nn.sigmoid(logit)
    hidden = []
    for ref in (up_ref, far_up_ref):
        up = jnp.dot(normed, ref[...], preferred_element_type=jnp.float32)
        hidden.append(jnp.maximum(up, 0.0).astype(jnp.bfloat16))
    out = jnp.dot(hidden[0], down_ref[...], preferred_element_type=jnp.float32)
    if summing:
        out = out + jnp.dot(hidden[1], far_down_refs[0][...], preferred_element_type=jnp.float32)
    else:
        count = len(firsts)
        near_refs, far_refs = far_down_refs[:count], far_down_refs[count:]
        group = lax.axis_index("groups")
        out = out + in_pieces(hidden[1], firsts, near_refs, far_refs, share, group)
    y = x + gate * out
    y_ref[...] = jnp.where(routes_ref[tick, 0, 0] == side, y, 0.0).astype(jnp.bfloat16)


def gather_kernel(first_ref, second_ref, own_ref, returned_ref, out_ref):
    out_ref[0, 0] = first_ref[...]
    out_ref[0, 1] = second_ref[...]
    total = own_ref[...].astype(jnp.float32) + returned_ref[...].astype(jnp.float32)
    out_ref[0, 2] = total.astype(jnp.bfloat16)


def pairs_per_device(
    pending_microgroups,
    arriving_microgroups,
    expert_choice_grid,
    rootmean_gain,
    gating_columns,
    up_projection_matrix,
    down_projection_matrix,
):
    splits = lax.axis_size("groups")
    places = lax.axis_size("expert")
    legs = lax.axis_size("section")
    own = (up_projection_matrix[0, 0], down_projection_matrix[0, 0])
    width, hid = own[0].shape
    num_rows = pending_microgroups.shape[1]
    share = width // splits
    pieces = piece_list(share)
    in_vmem = pl.BlockSpec(memory_space=pltpu.VMEM)
    anywhere = pl.BlockSpec(memory_space=pl.ANY)
    limited = pltpu.CompilerParams(vmem_limit_bytes=8 << 20)

    def cut(some):
        return pl.pallas_call(
            functools.partial(cut_kernel, some, share),
            out_shape=[jax.ShapeDtypeStruct((p[2], hid), jnp.bfloat16) for p in some],
            in_specs=[pl.BlockSpec(memory_space=pltpu.HBM)] * 2,
            out_specs=[in_vmem] * len(some),
            scratch_shapes=[pltpu.SemaphoreType.DMA((len(some),))],
            compiler_params=limited,
        )(*own)

    sending = [*cut(pieces[:1]), *cut(pieces[1:])]
    near, far = [], []
    for piece in sending:
        near.append(swapped(piece, "expert", 0))
    for piece in near:
        far.append(swapped(piece, "groups", 0))

    def join(m):
        chosen = [i for i, p in enumerate(pieces) if p[0] == m]
        return pl.pallas_call(
            functools.partial(join_kernel, [pieces[i][1] for i in chosen], share),
            out_shape=jax.ShapeDtypeStruct((width, hid), jnp.bfloat16),
            in_specs=[in_vmem] * (2 * len(chosen)),
            out_specs=in_vmem,
            compiler_params=limited,
        )(*[near[i] for i in chosen], *[far[i] for i in chosen])

    far_up = join(0)
    far_down = join(1)
    down_pieces = [i for i, p in enumerate(pieces) if p[0] == 1]
    firsts = [pieces[i][1] for i in down_pieces]
    down_parts = [near[i] for i in down_pieces] + [far[i] for i in down_pieces]

    columns = jnp.swapaxes(gating_columns[0], 0, 1)
    own_rows = pending_microgroups[0]
    other_rows = swapped(own_rows, "expert", 1)
    pairs = [(e * legs, (e ^ 2) * legs) for e in range(places)]
    fresh_other = lax.ppermute(arriving_microgroups, ("expert", "section"), pairs)
    fresh = (arriving_microgroups, fresh_other)
    rows_shape = jax.ShapeDtypeStruct((num_rows, width), jnp.bfloat16)

    def layer(tick, which, parts, after):
        summing = len(parts) == 2
        moving = summing and which == 0
        operands = [expert_choice_grid, *parts]
        if summing:
            operands.append(fresh[which])
        operands += [rootmean_gain, columns, *own, far_up]
        operands += [far_down] if summing else down_parts
        in_specs = [pl.BlockSpec(memory_space=pltpu.SMEM)] + [in_vmem] * (len(operands) - 1)
        outs = [rows_shape] * (2 if moving else 1)
        return pl.pallas_call(
            functools.partial(layer_kernel, tick, firsts, share, summing, moving),
            out_shape=outs,
            in_specs=[*in_specs, anywhere],
            out_specs=[in_vmem] * len(outs),
            compiler_params=pltpu.CompilerParams(vmem_limit_bytes=16 << 20),
        )(*operands, after)

    def ahead(value, flip, wrap):
        last = legs if wrap else legs - 1
        perm = [
            (e * legs + s, (e ^ flip) * legs + (s + 1) % legs)
            for e in range(places)
            for s in range(last)
        ]
        return lax.ppermute(value, ("expert", "section"), perm)

    def back(value):
        return lax.ppermute(value, "section", [((s + 1) % legs, s) for s in range(legs)])

    current = {0: (own_rows,), 1: (other_rows,)}
    outputs = []
    after = own_rows
    for tick in range(TICKS):
        following = {}
        straight = {}
        done = {}
        for which in chunk_order(tick):
            got = layer(tick, which, current[which], after)
            after = done[which] = got[0]
            if tick + 1 < TICKS:
                arrives = 1 - which
                following[arrives] = ahead(got[0], 2, arrives == 0)
                straight[which] = ahead(got[0], 0, which == 0)
            elif which == 1:
                returned = swapped(got[0], "expert", 1)
            if len(got) == 2:
                outputs.append(back(got[1]))
        if tick + 1 < TICKS:
            current = {w: (straight[w], following[w]) for w in (0, 1)}
    return pl.pallas_call(
        gather_kernel,
        out_shape=jax.ShapeDtypeStruct((1, TICKS, num_rows, width), jnp.bfloat16),
        in_specs=[in_vmem] * 4,
        out_specs=in_vmem,
        compiler_params=limited,
        name="gather",
    )(*outputs, done[0], returned)


def chunk_order(tick):
    return (1, 0) if (TICKS - 1 - tick) % 2 == 0 else (0, 1)


def solution(mesh):
    placed = (
        P("section", ("groups", "expert"), None),
        P(None, ("groups", "expert"), None),
        P(None, "section", ("groups", "expert")),
        P("section", None),
        P("section", None, None),
        P("section", "expert", None, None),
        P("section", "expert", None, None),
    )

    paired = mesh.shape["expert"] == 4 and mesh.shape["groups"] == 2

    def per_device(*args):
        if paired and args[4].shape[2] == 2:
            return pairs_per_device(*args)
        return slots_per_device(*args)

    return jax.shard_map(
        per_device,
        mesh=mesh,
        in_specs=placed,
        out_specs=P("section", None, ("groups", "expert"), None),
        check_vma=False,
    )
```

```python
import functools

import jax
import jax.numpy as jnp
from jax import lax
from jax.experimental import pallas as pl
from jax.experimental.pallas import tpu as pltpu
from jax.sharding import PartitionSpec as P


TICKS = 3


def swapped(x, axis, bit):
    return lax.ppermute(x, axis, [(i, i ^ 1 << bit) for i in range(lax.axis_size(axis))])


def from_behind(value, axis, steps):
    count = lax.axis_size(axis)
    initial, last = (max(0, -steps), min(count, count - steps))
    return lax.ppermute(value, axis, [(source, source + steps) for source in range(initial, last)])


def half_output(received, up_projection_matrix, down_projection_matrix):
    hidden = jnp.maximum(
        jnp.einsum(
            "sid,dh->sih", received, up_projection_matrix, preferred_element_type=jnp.float32
        ),
        0.0,
    ).astype(jnp.bfloat16)
    return jnp.einsum(
        "sih,hd->sid", hidden, down_projection_matrix, preferred_element_type=jnp.float32
    ).astype(jnp.bfloat16)


def expert_layer(
    tok_rows,
    routes,
    rootmean_gain,
    gating_columns,
    up_projection_matrix,
    down_projection_matrix,
    other_in,
    other_out,
):
    num_rows, width = tok_rows.shape
    experts = gating_columns.shape[1]
    capacity = min(num_rows, 3 * num_rows // experts)
    float_rows = tok_rows.astype(jnp.float32)
    inv_rms = lax.rsqrt(jnp.mean(float_rows * float_rows, axis=-1, keepdims=True) + 1e-06)
    normed = (float_rows * inv_rms * rootmean_gain).astype(jnp.bfloat16)
    logits = jnp.dot(normed, gating_columns, preferred_element_type=jnp.float32)
    one_hot = routes[:, None] == jnp.arange(experts, dtype=jnp.int32)[None, :]
    gate_value = jax.nn.sigmoid(jnp.sum(jnp.where(one_hot, logits, 0.0), axis=1))
    flags = one_hot.astype(jnp.int32)
    slot_rank = jnp.sum((jnp.cumsum(flags, axis=0) - flags) * flags, axis=1)
    slot_index = routes * capacity + slot_rank
    placing = (
        slot_index[None, :] == jnp.arange(experts * capacity, dtype=jnp.int32)[:, None]
    ).astype(jnp.bfloat16)
    outgoing = jnp.dot(placing, normed, preferred_element_type=jnp.float32).astype(jnp.bfloat16)
    outgoing = outgoing.reshape(experts, capacity, width)
    halves = outgoing.reshape(2 * experts, capacity // 2, width)
    received = lax.all_to_all(halves, "expert", split_axis=0, concat_axis=0, tiled=True)
    own_part = half_output(received, up_projection_matrix, down_projection_matrix)
    other_part = half_output(received, other_in, other_out)
    summed = (own_part.astype(jnp.float32) + other_part.astype(jnp.float32)).astype(jnp.bfloat16)
    combined = lax.all_to_all(summed, "expert", split_axis=0, concat_axis=0, tiled=True)
    flat_out = combined.reshape(experts * capacity, width)
    expert_out = lax.dot_general(
        placing, flat_out, (((0,), (0,)), ((), ())), preferred_element_type=jnp.float32
    )
    return (float_rows + gate_value[:, None] * expert_out).astype(jnp.bfloat16)


def slots_per_device(
    pending_microgroups,
    arriving_microgroups,
    expert_choice_grid,
    rootmean_gain,
    gating_columns,
    up_projection_matrix,
    down_projection_matrix,
):
    leg_position = lax.axis_index("section")
    own_in = up_projection_matrix[0, 0]
    own_out = down_projection_matrix[0, 0]
    other_in, other_out = swapped((own_in, own_out), "expert", 0)
    running_activation = pending_microgroups[0]
    per_tick = []
    for tick_idx in range(TICKS):
        layer_out = expert_layer(
            running_activation,
            expert_choice_grid[tick_idx, 0],
            rootmean_gain[0],
            gating_columns[0],
            own_in,
            own_out,
            other_in,
            other_out,
        )
        per_tick.append(layer_out)
        if tick_idx + 1 < TICKS:
            moved = from_behind(layer_out, "section", 1)
            running_activation = jnp.where(leg_position == 0, arriving_microgroups[tick_idx], moved)
    return jnp.stack(per_tick)[None]


def piece_list(width):
    third, half = width // 3, width // 6
    return [
        (0, 0, half, half + third),
        (0, half, third, half + third),
        (1, 0, third, third),
        (1, 2 * third, third, 0),
    ]


def cut_kernel(some, *refs):
    count = len(some)
    sources, outs, sems = refs[: -count - 1], refs[-count - 1 : -1], refs[-1]
    group = lax.axis_index("groups")
    copies = []
    for index, ((m, first, size, share), out) in enumerate(zip(some, outs)):
        rows = pl.ds(pl.multiple_of(group * share + first, 128), size)
        copies.append(pltpu.make_async_copy(sources[m].at[rows, :], out, sems.at[index]))
    for copy in copies:
        copy.start()
    for copy in copies:
        copy.wait()


def join_kernel(some, *refs):
    refs, out_ref = list(refs[:-1]), refs[-1]
    group = lax.axis_index("groups")
    for _, first, size, share in some:
        for part in (group, 1 - group) if share else (0,):
            rows = pl.ds(pl.multiple_of(part * share + first, 128), size)
            out_ref[rows, :] = refs.pop(0)[...]


def from_pieces(rows, some, refs):
    refs = list(refs)
    group = lax.axis_index("groups")
    total = 0.0
    for _, first, size, share in some:
        taken = [rows[:, first : first + size]]
        if share:
            other = rows[:, share + first : share + first + size]
            taken = [jnp.where(group == 0, *pair) for pair in ((*taken, other), (other, *taken))]
        for part in taken:
            total += jnp.dot(part, refs.pop(0)[...], preferred_element_type=jnp.float32)
    return total


def layer_kernel(tick, which, last_tick, some, *refs):
    refs = list(refs)
    take = refs.pop
    routes_ref = take(0)
    straight_ref = take(0)
    cross_ref = take(0) if tick else None
    fresh_ref = take(0) if which == 0 else None
    gain_ref, columns_ref, up_ref, down_ref, far_up_ref = [take(0) for _ in range(5)]
    far_down_refs = [take(0) for _ in range(1 if tick else sum(2 if p[3] else 1 for p in some))]
    take(0)
    y_ref = take(0)
    side = lax.axis_index("expert") // 2
    leg = lax.axis_index("section")
    x = straight_ref[...].astype(jnp.float32)
    if tick:
        x = x + cross_ref[...].astype(jnp.float32)
        if which == 0:
            take(0)[...] = x.astype(jnp.bfloat16)
            x = jnp.where(leg == 0, fresh_ref[tick - 1].astype(jnp.float32), x)
    inv_rms = lax.rsqrt(jnp.mean(x * x, axis=-1, keepdims=True) + 1e-06)
    normed = (x * inv_rms * gain_ref[...]).astype(jnp.bfloat16)
    columns = columns_ref[...].astype(jnp.float32)
    column = jnp.where(side == 0, columns[0:1], columns[1:2])
    logit = jnp.sum(normed.astype(jnp.float32) * column, axis=-1, keepdims=True)
    gate = jax.nn.sigmoid(logit)
    hidden = []
    for ref in (up_ref, far_up_ref):
        up = jnp.dot(normed, ref[...], preferred_element_type=jnp.float32)
        hidden.append(jnp.maximum(up, 0.0).astype(jnp.bfloat16))
    out = jnp.dot(hidden[0], down_ref[...], preferred_element_type=jnp.float32)
    if len(far_down_refs) == 1:
        out = out + jnp.dot(hidden[1], far_down_refs[0][...], preferred_element_type=jnp.float32)
    else:
        out = out + from_pieces(hidden[1], some, far_down_refs)
    y = x + gate * out
    y = jnp.where(routes_ref[tick, 0, 0] == side, y, 0.0).astype(jnp.bfloat16)
    y_ref[...] = y
    if which == 0 and tick < last_tick:
        take(0)[...] = jnp.where(leg == lax.axis_size("section") - 1, fresh_ref[tick], y)


def gather_kernel(first_ref, second_ref, own_ref, returned_ref, out_ref):
    out_ref[0, 0] = first_ref[...]
    out_ref[0, 1] = second_ref[...]
    total = own_ref[...].astype(jnp.float32) + returned_ref[...].astype(jnp.float32)
    out_ref[0, 2] = total.astype(jnp.bfloat16)


def pairs_per_device(
    pending_microgroups,
    arriving_microgroups,
    expert_choice_grid,
    rootmean_gain,
    gating_columns,
    up_projection_matrix,
    down_projection_matrix,
):
    places = lax.axis_size("expert")
    legs = lax.axis_size("section")
    own = (up_projection_matrix[0, 0], down_projection_matrix[0, 0])
    width, hid = own[0].shape
    num_rows = pending_microgroups.shape[1]
    pieces = piece_list(width)
    in_vmem = pl.BlockSpec(memory_space=pltpu.VMEM)
    anywhere = pl.BlockSpec(memory_space=pl.ANY)
    limited = pltpu.CompilerParams(vmem_limit_bytes=8 << 20)

    def cut(some):
        return pl.pallas_call(
            functools.partial(cut_kernel, some),
            out_shape=[jax.ShapeDtypeStruct((p[2], hid), jnp.bfloat16) for p in some],
            in_specs=[anywhere] * 2,
            out_specs=[CUT_OUT] * len(some),
            scratch_shapes=[pltpu.SemaphoreType.DMA((len(some),))],
            compiler_params=CUT_PARAMS,
        )(*own)

    sending = [*cut(pieces[:1]), *cut(pieces[1:])]
    near, parts = [], {}
    for piece in sending:
        near.append(swapped(piece, "expert", 0))
    for index, piece in enumerate(near):
        parts[index] = [piece]
        if pieces[index][3]:
            parts[index].append(swapped(piece, "groups", 0))
    by_matrix = [[i for i, p in enumerate(pieces) if p[0] == m] for m in (0, 1)]

    def join(m):
        operands = [part for i in by_matrix[m] for part in parts[i]]
        return pl.pallas_call(
            functools.partial(join_kernel, [pieces[i] for i in by_matrix[m]]),
            out_shape=jax.ShapeDtypeStruct((width, hid), jnp.bfloat16),
            in_specs=[in_vmem] * len(operands),
            out_specs=in_vmem,
            compiler_params=limited,
        )(*operands)

    far_up = join(0)
    far_down = join(1)
    down_some = [pieces[i] for i in by_matrix[1]]
    down_parts = [part for i in by_matrix[1] for part in parts[i]]

    columns = jnp.swapaxes(gating_columns[0], 0, 1)
    own_rows = pending_microgroups[0]
    other_rows = swapped(own_rows, "expert", 1)
    rows_shape = jax.ShapeDtypeStruct((num_rows, width), jnp.bfloat16)

    def layer(tick, which, inputs, after):
        operands = [expert_choice_grid, *inputs]
        if which == 0:
            operands.append(arriving_microgroups)
        operands += [rootmean_gain, columns, *own, far_up]
        operands += [far_down] if tick else down_parts
        in_specs = [pl.BlockSpec(memory_space=pltpu.SMEM)] + [in_vmem] * (len(operands) - 1)
        extras = (which == 0) * ((tick > 0) + (tick + 1 < TICKS))
        return pl.pallas_call(
            functools.partial(layer_kernel, tick, which, TICKS - 1, down_some),
            out_shape=[rows_shape] * (1 + extras),
            in_specs=[*in_specs, anywhere],
            out_specs=[in_vmem] * (1 + extras),
            compiler_params=pltpu.CompilerParams(vmem_limit_bytes=16 << 20),
        )(*operands, after)

    def ahead(value, flip, wrap):
        last = legs if wrap else legs - 1
        perm = [
            (e * legs + s, (e ^ flip) * legs + (s + 1) % legs)
            for e in range(places)
            for s in range(last)
        ]
        return lax.ppermute(value, ("expert", "section"), perm)

    def back(value):
        return lax.ppermute(value, "section", [((s + 1) % legs, s) for s in range(legs)])

    current = {0: (own_rows,), 1: (other_rows,)}
    outputs = []
    after = own_rows
    for tick in range(TICKS):
        following = {}
        straight = {}
        done = {}
        for which in chunk_order(tick):
            got = layer(tick, which, current[which], after)
            after = done[which] = got[0]
            if tick + 1 < TICKS:
                following[1 - which] = ahead(got[-1], 2, True)
                straight[which] = ahead(got[0], 0, which == 0)
            elif which == 1:
                returned = swapped(got[0], "expert", 1)
            if tick and which == 0:
                outputs.append(back(got[1]))
        if tick + 1 < TICKS:
            current = {w: (straight[w], following[w]) for w in (0, 1)}
    return pl.pallas_call(
        gather_kernel,
        out_shape=jax.ShapeDtypeStruct((1, TICKS, num_rows, width), jnp.bfloat16),
        in_specs=[in_vmem] * 4,
        out_specs=in_vmem,
        compiler_params=limited,
        name="gather",
    )(*outputs, done[0], returned)


CUT_OUT = pl.BlockSpec(memory_space=pltpu.VMEM)
CUT_PARAMS = pltpu.CompilerParams(vmem_limit_bytes=60 << 20)


def chunk_order(tick):
    return (1, 0) if (TICKS - 1 - tick) % 2 == 0 else (0, 1)


def solution(mesh):
    placed = (
        P("section", ("groups", "expert"), None),
        P(None, ("groups", "expert"), None),
        P(None, "section", ("groups", "expert")),
        P("section", None),
        P("section", None, None),
        P("section", "expert", None, None),
        P("section", "expert", None, None),
    )

    paired = mesh.shape["expert"] == 4 and mesh.shape["groups"] == 2

    def per_device(*args):
        if paired and args[4].shape[2] == 2 and args[5].shape[2] % 768 == 0:
            return pairs_per_device(*args)
        return slots_per_device(*args)

    return jax.shard_map(
        per_device,
        mesh=mesh,
        in_specs=placed,
        out_specs=P("section", None, ("groups", "expert"), None),
        check_vma=False,
    )
```

```python
import functools

import jax
import jax.numpy as jnp
from jax import lax
from jax.experimental import pallas as pl
from jax.experimental.pallas import tpu as pltpu
from jax.sharding import PartitionSpec as P


TICKS = 3


def swapped(x, axis, bit):
    return lax.ppermute(x, axis, [(i, i ^ 1 << bit) for i in range(lax.axis_size(axis))])


def from_behind(value, axis, steps):
    count = lax.axis_size(axis)
    initial, last = (max(0, -steps), min(count, count - steps))
    return lax.ppermute(value, axis, [(source, source + steps) for source in range(initial, last)])


def half_output(received, up_projection_matrix, down_projection_matrix):
    hidden = jnp.maximum(
        jnp.einsum(
            "sid,dh->sih", received, up_projection_matrix, preferred_element_type=jnp.float32
        ),
        0.0,
    ).astype(jnp.bfloat16)
    return jnp.einsum(
        "sih,hd->sid", hidden, down_projection_matrix, preferred_element_type=jnp.float32
    ).astype(jnp.bfloat16)


def expert_layer(
    tok_rows,
    routes,
    rootmean_gain,
    gating_columns,
    up_projection_matrix,
    down_projection_matrix,
    other_in,
    other_out,
):
    num_rows, width = tok_rows.shape
    experts = gating_columns.shape[1]
    capacity = min(num_rows, 3 * num_rows // experts)
    float_rows = tok_rows.astype(jnp.float32)
    inv_rms = lax.rsqrt(jnp.mean(float_rows * float_rows, axis=-1, keepdims=True) + 1e-06)
    normed = (float_rows * inv_rms * rootmean_gain).astype(jnp.bfloat16)
    logits = jnp.dot(normed, gating_columns, preferred_element_type=jnp.float32)
    one_hot = routes[:, None] == jnp.arange(experts, dtype=jnp.int32)[None, :]
    gate_value = jax.nn.sigmoid(jnp.sum(jnp.where(one_hot, logits, 0.0), axis=1))
    flags = one_hot.astype(jnp.int32)
    slot_rank = jnp.sum((jnp.cumsum(flags, axis=0) - flags) * flags, axis=1)
    slot_index = routes * capacity + slot_rank
    placing = (
        slot_index[None, :] == jnp.arange(experts * capacity, dtype=jnp.int32)[:, None]
    ).astype(jnp.bfloat16)
    outgoing = jnp.dot(placing, normed, preferred_element_type=jnp.float32).astype(jnp.bfloat16)
    outgoing = outgoing.reshape(experts, capacity, width)
    halves = outgoing.reshape(2 * experts, capacity // 2, width)
    received = lax.all_to_all(halves, "expert", split_axis=0, concat_axis=0, tiled=True)
    own_part = half_output(received, up_projection_matrix, down_projection_matrix)
    other_part = half_output(received, other_in, other_out)
    summed = (own_part.astype(jnp.float32) + other_part.astype(jnp.float32)).astype(jnp.bfloat16)
    combined = lax.all_to_all(summed, "expert", split_axis=0, concat_axis=0, tiled=True)
    flat_out = combined.reshape(experts * capacity, width)
    expert_out = lax.dot_general(
        placing, flat_out, (((0,), (0,)), ((), ())), preferred_element_type=jnp.float32
    )
    return (float_rows + gate_value[:, None] * expert_out).astype(jnp.bfloat16)


def slots_per_device(
    pending_microgroups,
    arriving_microgroups,
    expert_choice_grid,
    rootmean_gain,
    gating_columns,
    up_projection_matrix,
    down_projection_matrix,
):
    leg_position = lax.axis_index("section")
    own_in = up_projection_matrix[0, 0]
    own_out = down_projection_matrix[0, 0]
    other_in, other_out = swapped((own_in, own_out), "expert", 0)
    running_activation = pending_microgroups[0]
    per_tick = []
    for tick_idx in range(TICKS):
        layer_out = expert_layer(
            running_activation,
            expert_choice_grid[tick_idx, 0],
            rootmean_gain[0],
            gating_columns[0],
            own_in,
            own_out,
            other_in,
            other_out,
        )
        per_tick.append(layer_out)
        if tick_idx + 1 < TICKS:
            moved = from_behind(layer_out, "section", 1)
            running_activation = jnp.where(leg_position == 0, arriving_microgroups[tick_idx], moved)
    return jnp.stack(per_tick)[None]


def piece_list(width):
    direct = width // 8
    pieces = []
    for m, share in ((0, width // 2), (1, (width - direct) // 2)):
        pieces += [(m, r * (share // 3), share // 3, share) for r in range(3)]
    return [*pieces, (1, width - direct, direct, 0)]


def cut_kernel(some, *refs):
    count = len(some)
    sources, outs, sems = refs[: -count - 1], refs[-count - 1 : -1], refs[-1]
    group = lax.axis_index("groups")
    copies = []
    for index, ((m, first, size, share), out) in enumerate(zip(some, outs)):
        rows = pl.ds(pl.multiple_of(group * share + first, 16), size)
        copies.append(pltpu.make_async_copy(sources[m].at[rows, :], out, sems.at[index]))
    for copy in copies:
        copy.start()
    for copy in copies:
        copy.wait()


def join_kernel(some, *refs):
    refs, out_ref = list(refs[:-1]), refs[-1]
    group = lax.axis_index("groups")
    for _, first, size, share in some:
        for part in (group, 1 - group) if share else (0,):
            rows = pl.ds(pl.multiple_of(part * share + first, 16), size)
            out_ref[rows, :] = refs.pop(0)[...]


HOT_0, OWN_FIRST, WAS_HOT, IS_HOT, FLIP_IN, FLIP_OUT, HOT_2, FLIP_2 = range(8)


def table_kernel(here_ref, next_ref, second_ref, behind_ref, table_ref):
    side = lax.axis_index("expert") // 2
    leg = lax.axis_index("section")
    legs = lax.axis_size("section")

    def differ(one, other):
        return (one != other).astype(jnp.int32)

    def hot(ref, tick):
        return ref[tick, 0, 0]

    flip_in = differ(hot(here_ref, 0), hot(next_ref, 1))
    flip_out = jnp.where(leg == legs - 2, 0, differ(hot(next_ref, 1), hot(second_ref, 2)))
    table_ref[HOT_0] = 1 - differ(hot(here_ref, 0), side)
    table_ref[OWN_FIRST] = flip_in * (1 - flip_out)
    table_ref[WAS_HOT] = 1 - differ(hot(behind_ref, 0), side)
    table_ref[IS_HOT] = 1 - differ(hot(here_ref, 1), side)
    table_ref[FLIP_IN] = differ(hot(behind_ref, 0), hot(here_ref, 1))
    table_ref[FLIP_OUT] = jnp.where(
        leg == legs - 1, 0, differ(hot(here_ref, 1), hot(next_ref, 2))
    )
    table_ref[HOT_2] = 1 - differ(hot(here_ref, 2), side)
    table_ref[FLIP_2] = jnp.where(leg == 0, 0, differ(hot(behind_ref, 1), hot(here_ref, 2)))


def expert_rows(x, gain_ref, columns_ref, up_ref, down_ref, far_up_ref, far_down_ref):
    x = x.astype(jnp.float32)
    inv_rms = lax.rsqrt(jnp.mean(x * x, axis=-1, keepdims=True) + 1e-06)
    normed = (x * inv_rms * gain_ref[...]).astype(jnp.bfloat16)
    columns = columns_ref[...].astype(jnp.float32)
    column = jnp.where(lax.axis_index("expert") // 2 == 0, columns[0:1], columns[1:2])
    logit = jnp.sum(normed.astype(jnp.float32) * column, axis=-1, keepdims=True)
    out = 0.0
    for into, outof in ((up_ref, down_ref), (far_up_ref, far_down_ref)):
        up = jnp.dot(normed, into[...], preferred_element_type=jnp.float32)
        hidden = jnp.maximum(up, 0.0).astype(jnp.bfloat16)
        out += jnp.dot(hidden, outof[...], preferred_element_type=jnp.float32)
    return (x + jax.nn.sigmoid(logit) * out).astype(jnp.bfloat16)


def choose(flag, one, other):
    return jnp.where(flag, one, other)


def at_first():
    return lax.axis_index("section") == 0


def tick_0(half, table_ref, own_ref, partner_ref, fresh_ref, *refs):
    *weights, _, both_ref, sent_ref = refs
    size = sent_ref.shape[0]
    rows = pl.ds(half * size, size)
    y = expert_rows(jnp.concatenate([own_ref[rows], partner_ref[rows]]), *weights)
    both_ref[...] = y
    last = lax.axis_index("section") == lax.axis_size("section") - 1
    own = choose(last, fresh_ref[0, rows], y[:size])
    partner_first = (table_ref[HOT_0] != 0) & (table_ref[OWN_FIRST] == 0)
    sent_ref[...] = choose(partner_first, y[size:], own)


def tick_1_before(half, table_ref, straight_ref, first_ref, fresh_ref, *refs):
    *weights, _, y_ref, sent_ref = refs
    size = sent_ref.shape[0]
    flip_in, flip_out = table_ref[FLIP_IN] != 0, table_ref[FLIP_OUT] != 0
    own, partner, first = straight_ref[:size], straight_ref[size:], first_ref[...]
    fresh = fresh_ref[0, pl.ds(half * size, size)]
    own_in = choose(at_first(), fresh, choose(flip_in, first, own))
    partner_in = choose(flip_in | at_first(), first, partner)
    y = expert_rows(choose(flip_out, own_in, partner_in), *weights)
    y_ref[...] = y
    waiting = choose(flip_out, choose(at_first(), fresh, own), partner)
    sent_ref[...] = choose(table_ref[IS_HOT] != 0, y, waiting)


def tick_1_after(
    half, table_ref, straight_ref, first_ref, second_ref, done_ref, fresh_ref, *refs
):
    *weights, _, both_ref, was_ref, is_ref = refs
    size = was_ref.shape[0]
    flip_in, flip_out = table_ref[FLIP_IN] != 0, table_ref[FLIP_OUT] != 0
    is_hot = table_ref[IS_HOT] != 0
    own, partner = straight_ref[:size], straight_ref[size:]
    first, second, done = first_ref[...], second_ref[...], done_ref[...]
    fresh = fresh_ref[0, pl.ds(half * size, size)]
    partner_in = choose(flip_in, second, choose(at_first(), first, partner))
    own_in = choose(at_first(), fresh, choose(flip_in, second, own))
    y = expert_rows(choose(flip_out, partner_in, own_in), *weights)
    both_ref[:size] = choose(is_hot, done, second)
    both_ref[size:] = y
    arrived = choose(flip_in & ~flip_out, second, first)
    was_ref[...] = choose(table_ref[WAS_HOT] != 0, own, arrived)
    is_ref[...] = choose(is_hot, choose(flip_out, done, y), second)


def tick_2_before(half, table_ref, straight_ref, fresh_ref, *refs):
    *weights, _, sent_ref = refs
    size = sent_ref.shape[0]
    fresh = fresh_ref[pl.ds(half * size, size)]
    y = expert_rows(choose(at_first(), fresh, straight_ref[:size]), *weights)
    sent_ref[...] = choose(table_ref[HOT_2] != 0, y, straight_ref[size:])


def tick_2_after(half, table_ref, straight_ref, third_ref, fresh_ref, *refs):
    *weights, _, out_ref = refs
    size = out_ref.shape[0]
    third = third_ref[...]
    fresh = fresh_ref[1, pl.ds(half * size, size)]
    x = choose(table_ref[FLIP_2] != 0, third, straight_ref[size:])
    y = expert_rows(choose(at_first(), fresh, x), *weights)
    out_ref[...] = choose(table_ref[HOT_2] != 0, y, third)


def gather_kernel(table_ref, *refs):
    *refs, out_ref = refs
    size = refs[0].shape[0]
    late = (table_ref[FLIP_OUT] != 0) & (table_ref[IS_HOT] == 0)
    for half, (was, here, back, last) in enumerate(zip(*[iter(refs)] * 4)):
        rows = pl.ds(half * size, size)
        out_ref[0, 0, rows] = was[...]
        out_ref[0, 1, rows] = choose(late, back[...], here[...])
        out_ref[0, 2, rows] = last[...]


def pairs_per_device(
    pending_microgroups,
    arriving_microgroups,
    expert_choice_grid,
    rootmean_gain,
    gating_columns,
    up_projection_matrix,
    down_projection_matrix,
):
    places = lax.axis_size("expert")
    legs = lax.axis_size("section")
    own = (up_projection_matrix[0, 0], down_projection_matrix[0, 0])
    width, hid = own[0].shape
    num_rows = pending_microgroups.shape[1]
    size = num_rows // 2
    pieces = piece_list(width)
    in_vmem = pl.BlockSpec(memory_space=pltpu.VMEM)
    in_smem = pl.BlockSpec(memory_space=pltpu.SMEM)
    anywhere = pl.BlockSpec(memory_space=pl.ANY)
    limited = pltpu.CompilerParams(vmem_limit_bytes=8 << 20)

    def rows_of(count):
        return jax.ShapeDtypeStruct((count, width), jnp.bfloat16)

    def turned(value, axis, steps):
        count = lax.axis_size(axis)
        return lax.ppermute(value, axis, [((i + steps) % count, i) for i in range(count)])

    def cut(some):
        return pl.pallas_call(
            functools.partial(cut_kernel, some),
            out_shape=[jax.ShapeDtypeStruct((p[2], hid), jnp.bfloat16) for p in some],
            in_specs=[anywhere] * 2,
            out_specs=[in_vmem] * len(some),
            scratch_shapes=[pltpu.SemaphoreType.DMA((len(some),))],
            compiler_params=pltpu.CompilerParams(vmem_limit_bytes=60 << 20),
        )(*own)

    sending = [*cut(pieces[:1]), *cut(pieces[1:])]
    near = [swapped(piece, "expert", 0) for piece in sending]
    parts = [
        [piece, swapped(piece, "groups", 0)] if pieces[i][3] else [piece]
        for i, piece in enumerate(near)
    ]

    def join(m):
        chosen = [i for i, p in enumerate(pieces) if p[0] == m]
        operands = [part for i in chosen for part in parts[i]]
        return pl.pallas_call(
            functools.partial(join_kernel, [pieces[i] for i in chosen]),
            out_shape=jax.ShapeDtypeStruct((width, hid), jnp.bfloat16),
            in_specs=[in_vmem] * len(operands),
            out_specs=in_vmem,
            compiler_params=limited,
        )(*operands)

    routes = [expert_choice_grid]
    routes += [turned(expert_choice_grid, "section", k) for k in (1, 2, legs - 1)]
    table = pl.pallas_call(
        table_kernel,
        out_shape=jax.ShapeDtypeStruct((8,), jnp.int32),
        in_specs=[in_smem] * 4,
        out_specs=in_smem,
        compiler_params=limited,
        name="table",
    )(*routes)

    columns = jnp.swapaxes(gating_columns[0], 0, 1)
    weights = [rootmean_gain, columns, *own, join(0), join(1)]
    own_rows = pending_microgroups[0]
    other_rows = swapped(own_rows, "expert", 1)
    pairs = [(e * legs, (e ^ 2) * legs) for e in range(places)]
    fresh_other = lax.ppermute(arriving_microgroups[1], ("expert", "section"), pairs)

    after = [own_rows]

    def stage(body, half, inputs, outs):
        operands = [table, *inputs, *weights]
        got = pl.pallas_call(
            functools.partial(body, half),
            out_shape=[rows_of(count) for count in outs],
            in_specs=[in_smem, *[in_vmem] * (len(operands) - 1), anywhere],
            out_specs=[in_vmem] * len(outs),
            compiler_params=pltpu.CompilerParams(vmem_limit_bytes=16 << 20),
        )(*operands, after[-1])
        after.append(got[0])
        return got

    def ahead(value, flip, wrap):
        last = legs if wrap else legs - 1
        perm = [
            (e * legs + s, (e ^ flip) * legs + (s + 1) % legs)
            for e in range(places)
            for s in range(last)
        ]
        return lax.ppermute(value, ("expert", "section"), perm)

    halves = (0, 1)
    straight, first, second, third = [None] * 2, [None] * 2, [None] * 2, [None] * 2
    done, was, here, back, last = [None] * 2, [None] * 2, [None] * 2, [None] * 2, [None] * 2
    for h in halves:
        both, sent = stage(tick_0, h, [own_rows, other_rows, arriving_microgroups], (2 * size, size))
        first[h] = ahead(sent, 2, True)
        straight[h] = ahead(both, 0, True)
    for h in halves:
        inputs = [straight[h], first[h], arriving_microgroups]
        done[h], sent = stage(tick_1_before, h, inputs, (size, size))
        second[h] = swapped(sent, "expert", 1)
    for h in halves:
        inputs = [straight[h], first[h], second[h], done[h], arriving_microgroups]
        both, was[h], here[h] = stage(tick_1_after, h, inputs, (2 * size, size, size))
        straight[h] = ahead(both, 0, False)
        was[h] = turned(was[h], "section", 1)
    for h in halves:
        (sent,) = stage(tick_2_before, h, [straight[h], fresh_other], (size,))
        third[h] = swapped(sent, "expert", 1)
    for h in halves:
        back[h] = turned(third[h], "section", 1)
        (last[h],) = stage(tick_2_after, h, [straight[h], third[h], arriving_microgroups], (size,))
    operands = [part for h in halves for part in (was[h], here[h], back[h], last[h])]
    return pl.pallas_call(
        gather_kernel,
        out_shape=jax.ShapeDtypeStruct((1, TICKS, num_rows, width), jnp.bfloat16),
        in_specs=[in_smem, *[in_vmem] * len(operands)],
        out_specs=in_vmem,
        compiler_params=limited,
        name="gather",
    )(table, *operands)


def solution(mesh):
    placed = (
        P("section", ("groups", "expert"), None),
        P(None, ("groups", "expert"), None),
        P(None, "section", ("groups", "expert")),
        P("section", None),
        P("section", None, None),
        P("section", "expert", None, None),
        P("section", "expert", None, None),
    )

    paired = mesh.shape["expert"] == 4 and mesh.shape["groups"] == 2 and mesh.shape["section"] > 2

    def per_device(*args):
        if paired and args[4].shape[2] == 2 and args[5].shape[2] % 768 == 0:
            return pairs_per_device(*args)
        return slots_per_device(*args)

    return jax.shard_map(
        per_device,
        mesh=mesh,
        in_specs=placed,
        out_specs=P("section", None, ("groups", "expert"), None),
        check_vma=False,
    )
```

```python
import functools

import jax
import jax.numpy as jnp
from jax import lax
from jax.experimental import pallas as pl
from jax.experimental.pallas import tpu as pltpu
from jax.sharding import PartitionSpec as P


TICKS = 3


def swapped(x, axis, bit):
    return lax.ppermute(x, axis, [(i, i ^ 1 << bit) for i in range(lax.axis_size(axis))])


def from_behind(value, axis, steps):
    count = lax.axis_size(axis)
    initial, last = (max(0, -steps), min(count, count - steps))
    return lax.ppermute(value, axis, [(source, source + steps) for source in range(initial, last)])


def half_output(received, up_projection_matrix, down_projection_matrix):
    hidden = jnp.maximum(
        jnp.einsum(
            "sid,dh->sih", received, up_projection_matrix, preferred_element_type=jnp.float32
        ),
        0.0,
    ).astype(jnp.bfloat16)
    return jnp.einsum(
        "sih,hd->sid", hidden, down_projection_matrix, preferred_element_type=jnp.float32
    ).astype(jnp.bfloat16)


def expert_layer(
    tok_rows,
    routes,
    rootmean_gain,
    gating_columns,
    up_projection_matrix,
    down_projection_matrix,
    other_in,
    other_out,
):
    num_rows, width = tok_rows.shape
    experts = gating_columns.shape[1]
    capacity = min(num_rows, 3 * num_rows // experts)
    float_rows = tok_rows.astype(jnp.float32)
    inv_rms = lax.rsqrt(jnp.mean(float_rows * float_rows, axis=-1, keepdims=True) + 1e-06)
    normed = (float_rows * inv_rms * rootmean_gain).astype(jnp.bfloat16)
    logits = jnp.dot(normed, gating_columns, preferred_element_type=jnp.float32)
    one_hot = routes[:, None] == jnp.arange(experts, dtype=jnp.int32)[None, :]
    gate_value = jax.nn.sigmoid(jnp.sum(jnp.where(one_hot, logits, 0.0), axis=1))
    flags = one_hot.astype(jnp.int32)
    slot_rank = jnp.sum((jnp.cumsum(flags, axis=0) - flags) * flags, axis=1)
    slot_index = routes * capacity + slot_rank
    placing = (
        slot_index[None, :] == jnp.arange(experts * capacity, dtype=jnp.int32)[:, None]
    ).astype(jnp.bfloat16)
    outgoing = jnp.dot(placing, normed, preferred_element_type=jnp.float32).astype(jnp.bfloat16)
    outgoing = outgoing.reshape(experts, capacity, width)
    halves = outgoing.reshape(2 * experts, capacity // 2, width)
    received = lax.all_to_all(halves, "expert", split_axis=0, concat_axis=0, tiled=True)
    own_part = half_output(received, up_projection_matrix, down_projection_matrix)
    other_part = half_output(received, other_in, other_out)
    summed = (own_part.astype(jnp.float32) + other_part.astype(jnp.float32)).astype(jnp.bfloat16)
    combined = lax.all_to_all(summed, "expert", split_axis=0, concat_axis=0, tiled=True)
    flat_out = combined.reshape(experts * capacity, width)
    expert_out = lax.dot_general(
        placing, flat_out, (((0,), (0,)), ((), ())), preferred_element_type=jnp.float32
    )
    return (float_rows + gate_value[:, None] * expert_out).astype(jnp.bfloat16)


def slots_per_device(
    pending_microgroups,
    arriving_microgroups,
    expert_choice_grid,
    rootmean_gain,
    gating_columns,
    up_projection_matrix,
    down_projection_matrix,
):
    leg_position = lax.axis_index("section")
    own_in = up_projection_matrix[0, 0]
    own_out = down_projection_matrix[0, 0]
    other_in, other_out = swapped((own_in, own_out), "expert", 0)
    running_activation = pending_microgroups[0]
    per_tick = []
    for tick_idx in range(TICKS):
        layer_out = expert_layer(
            running_activation,
            expert_choice_grid[tick_idx, 0],
            rootmean_gain[0],
            gating_columns[0],
            own_in,
            own_out,
            other_in,
            other_out,
        )
        per_tick.append(layer_out)
        if tick_idx + 1 < TICKS:
            moved = from_behind(layer_out, "section", 1)
            running_activation = jnp.where(leg_position == 0, arriving_microgroups[tick_idx], moved)
    return jnp.stack(per_tick)[None]


def piece_list(width):
    direct = width // 8
    pieces = []
    for m, share in ((0, width // 2), (1, (width - direct) // 2)):
        pieces += [(m, r * (share // 3), share // 3, share) for r in range(3)]
    return [*pieces, (1, width - direct, direct, 0)]


def cut_kernel(some, *refs):
    count = len(some)
    sources, outs, sems = refs[: -count - 1], refs[-count - 1 : -1], refs[-1]
    group = lax.axis_index("groups")
    copies = []
    for index, ((m, first, size, share), out) in enumerate(zip(some, outs)):
        rows = pl.ds(pl.multiple_of(group * share + first, 16), size)
        copies.append(pltpu.make_async_copy(sources[m].at[rows, :], out, sems.at[index]))
    for copy in copies:
        copy.start()
    for copy in copies:
        copy.wait()


def join_kernel(some, *refs):
    refs, out_ref = list(refs[:-1]), refs[-1]
    group = lax.axis_index("groups")
    for _, first, size, share in some:
        for part in (group, 1 - group) if share else (0,):
            rows = pl.ds(pl.multiple_of(part * share + first, 16), size)
            out_ref[rows, :] = refs.pop(0)[...]


PARTNER_FIRST, WAS_HOT, IS_HOT, FLIP_IN, FLIP_OUT, LATE, HOT_2, FLIP_2 = range(8)


def table_kernel(here_ref, next_ref, second_ref, behind_ref, *refs):
    table_ref = refs[-1]
    side = lax.axis_index("expert") // 2
    leg = lax.axis_index("section")
    legs = lax.axis_size("section")

    def differ(one, other):
        return (one != other).astype(jnp.int32)

    def hot(ref, tick):
        return ref[tick, 0, 0]

    def write(row, value):
        table_ref[row : row + 1] = jnp.full((1, table_ref.shape[1]), value, jnp.int32)

    flip_in = differ(hot(here_ref, 0), hot(next_ref, 1))
    flip_out = jnp.where(leg == legs - 2, 0, differ(hot(next_ref, 1), hot(second_ref, 2)))
    own_first = flip_in * (1 - flip_out)
    write(PARTNER_FIRST, (1 - differ(hot(here_ref, 0), side)) * (1 - own_first))
    flip_in = differ(hot(behind_ref, 0), hot(here_ref, 1))
    flip_out = jnp.where(leg == legs - 1, 0, differ(hot(here_ref, 1), hot(next_ref, 2)))
    is_hot = 1 - differ(hot(here_ref, 1), side)
    write(WAS_HOT, 1 - differ(hot(behind_ref, 0), side))
    write(IS_HOT, is_hot)
    write(FLIP_IN, flip_in)
    write(FLIP_OUT, flip_out)
    write(LATE, flip_out * (1 - is_hot))
    write(HOT_2, 1 - differ(hot(here_ref, 2), side))
    write(FLIP_2, jnp.where(leg == 0, 0, differ(hot(behind_ref, 1), hot(here_ref, 2))))


def expert_rows(x, gain_ref, columns_ref, up_ref, down_ref, far_up_ref, far_down_ref):
    x = x.astype(jnp.float32)
    inv_rms = lax.rsqrt(jnp.mean(x * x, axis=-1, keepdims=True) + 1e-06)
    normed = (x * inv_rms * gain_ref[...]).astype(jnp.bfloat16)
    columns = columns_ref[...].astype(jnp.float32)
    column = jnp.where(lax.axis_index("expert") // 2 == 0, columns[0:1], columns[1:2])
    logit = jnp.sum(normed.astype(jnp.float32) * column, axis=-1, keepdims=True)
    out = 0.0
    for into, outof in ((up_ref, down_ref), (far_up_ref, far_down_ref)):
        up = jnp.dot(normed, into[...], preferred_element_type=jnp.float32)
        hidden = jnp.maximum(up, 0.0).astype(jnp.bfloat16)
        out += jnp.dot(hidden, outof[...], preferred_element_type=jnp.float32)
    return (x + jax.nn.sigmoid(logit) * out).astype(jnp.bfloat16)


def flag(table_ref, row):
    return table_ref[row : row + 1, :1]


def choose(chosen, one, other):
    return jnp.where(chosen != 0, one, other)


def at_first():
    return lax.axis_index("section") == 0


def tick_0(table_ref, own_ref, partner_ref, fresh_ref, *refs):
    *weights, _, both_ref, first_ref, second_ref = refs
    count, size = own_ref.shape[0], first_ref.shape[0]
    y = expert_rows(jnp.concatenate([own_ref[...], partner_ref[...]]), *weights)
    both_ref[...] = y
    last = lax.axis_index("section") == lax.axis_size("section") - 1
    own = jnp.where(last, fresh_ref[0], y[:count])
    sent = choose(flag(table_ref, PARTNER_FIRST), y[count:], own)
    first_ref[...] = sent[:size]
    second_ref[...] = sent[size:]


def halves_of(straight_ref, half, size):
    count = straight_ref.shape[0] // 2
    rows = pl.ds(half * size, size)
    return straight_ref[rows], straight_ref[pl.ds(count + half * size, size)]


def tick_1_before(half, table_ref, straight_ref, first_ref, fresh_ref, *refs):
    *weights, _, y_ref, sent_ref = refs
    size = sent_ref.shape[0]
    flip_in, flip_out = flag(table_ref, FLIP_IN), flag(table_ref, FLIP_OUT)
    own, partner = halves_of(straight_ref, half, size)
    first = first_ref[...]
    fresh = fresh_ref[0, pl.ds(half * size, size)]
    own_in = jnp.where(at_first(), fresh, choose(flip_in, first, own))
    partner_in = jnp.where(at_first(), first, choose(flip_in, first, partner))
    y = expert_rows(choose(flip_out, own_in, partner_in), *weights)
    y_ref[...] = y
    waiting = choose(flip_out, jnp.where(at_first(), fresh, own), partner)
    sent_ref[...] = choose(flag(table_ref, IS_HOT), y, waiting)


def tick_1_after(half, table_ref, straight_ref, done_ref, fresh_ref, *refs):
    first_refs, second_refs = refs[: half + 1], refs[half + 1 : 2 * half + 2]
    *weights, _, both_ref, is_ref = refs[2 * half + 2 : len(refs) - half]
    size = is_ref.shape[0]
    flip_in, flip_out = flag(table_ref, FLIP_IN), flag(table_ref, FLIP_OUT)
    is_hot = flag(table_ref, IS_HOT)
    own, partner = halves_of(straight_ref, half, size)
    first, second, done = first_refs[half][...], second_refs[half][...], done_ref[...]
    fresh = fresh_ref[0, pl.ds(half * size, size)]
    partner_in = choose(flip_in, second, jnp.where(at_first(), first, partner))
    own_in = jnp.where(at_first(), fresh, choose(flip_in, second, own))
    y = expert_rows(choose(flip_out, partner_in, own_in), *weights)
    both_ref[:size] = choose(is_hot, done, second)
    both_ref[size:] = y
    is_ref[...] = choose(is_hot, choose(flip_out, done, y), second)
    if half:
        was_ref = refs[-1]
        swapped_in = flip_in * (1 - flip_out)
        for part in range(half + 1):
            own, _ = halves_of(straight_ref, part, size)
            arrived = choose(swapped_in, second_refs[part][...], first_refs[part][...])
            was_ref[pl.ds(part * size, size)] = choose(flag(table_ref, WAS_HOT), own, arrived)


def tick_2_before(half, table_ref, straight_ref, fresh_ref, *refs):
    *weights, _, sent_ref = refs
    size = sent_ref.shape[0]
    fresh = fresh_ref[pl.ds(half * size, size)]
    y = expert_rows(jnp.where(at_first(), fresh, straight_ref[:size]), *weights)
    sent_ref[...] = choose(flag(table_ref, HOT_2), y, straight_ref[size:])


def tick_2_after(half, table_ref, straight_ref, third_ref, fresh_ref, *refs):
    *weights, _, out_ref = refs
    size = out_ref.shape[0]
    third = third_ref[...]
    fresh = fresh_ref[1, pl.ds(half * size, size)]
    x = choose(flag(table_ref, FLIP_2), third, straight_ref[size:])
    y = expert_rows(jnp.where(at_first(), fresh, x), *weights)
    out_ref[...] = choose(flag(table_ref, HOT_2), y, third)


def gather_kernel(table_ref, was_ref, *refs):
    *refs, out_ref = refs
    size = refs[0].shape[0]
    out_ref[0, 0] = was_ref[...]
    for half, (here, back, last) in enumerate(zip(*[iter(refs)] * 3)):
        rows = pl.ds(half * size, size)
        out_ref[0, 1, rows] = choose(flag(table_ref, LATE), back[...], here[...])
        out_ref[0, 2, rows] = last[...]


def pairs_per_device(
    pending_microgroups,
    arriving_microgroups,
    expert_choice_grid,
    rootmean_gain,
    gating_columns,
    up_projection_matrix,
    down_projection_matrix,
):
    places = lax.axis_size("expert")
    legs = lax.axis_size("section")
    own = (up_projection_matrix[0, 0], down_projection_matrix[0, 0])
    width, hid = own[0].shape
    num_rows = pending_microgroups.shape[1]
    size = num_rows // 2
    pieces = piece_list(width)
    in_vmem = pl.BlockSpec(memory_space=pltpu.VMEM)
    in_smem = pl.BlockSpec(memory_space=pltpu.SMEM)
    anywhere = pl.BlockSpec(memory_space=pl.ANY)
    limited = pltpu.CompilerParams(vmem_limit_bytes=8 << 20)

    def rows_of(count):
        return jax.ShapeDtypeStruct((count, width), jnp.bfloat16)

    def turned(value, axis, steps):
        count = lax.axis_size(axis)
        return lax.ppermute(value, axis, [((i + steps) % count, i) for i in range(count)])

    def cut(some):
        return pl.pallas_call(
            functools.partial(cut_kernel, some),
            out_shape=[jax.ShapeDtypeStruct((p[2], hid), jnp.bfloat16) for p in some],
            in_specs=[anywhere] * 2,
            out_specs=[in_vmem] * len(some),
            scratch_shapes=[pltpu.SemaphoreType.DMA((len(some),))],
            compiler_params=pltpu.CompilerParams(vmem_limit_bytes=60 << 20),
        )(*own)

    sending = [*cut(pieces[:1]), *cut(pieces[1:])]
    near = [swapped(piece, "expert", 0) for piece in sending]
    parts = [
        [piece, swapped(piece, "groups", 0)] if pieces[i][3] else [piece]
        for i, piece in enumerate(near)
    ]

    def join(m):
        chosen = [i for i, p in enumerate(pieces) if p[0] == m]
        operands = [part for i in chosen for part in parts[i]]
        return pl.pallas_call(
            functools.partial(join_kernel, [pieces[i] for i in chosen]),
            out_shape=jax.ShapeDtypeStruct((width, hid), jnp.bfloat16),
            in_specs=[in_vmem] * len(operands),
            out_specs=in_vmem,
            compiler_params=limited,
        )(*operands)

    columns = jnp.swapaxes(gating_columns[0], 0, 1)
    routes = [expert_choice_grid]
    routes += [turned(expert_choice_grid, "section", k) for k in (1, 2, legs - 1)]
    table = pl.pallas_call(
        table_kernel,
        out_shape=jax.ShapeDtypeStruct((8, 128), jnp.int32),
        in_specs=[in_smem] * 4 + [in_vmem] * 5,
        out_specs=in_vmem,
        compiler_params=limited,
        name="table",
    )(*routes, *own, rootmean_gain, columns, arriving_microgroups)

    weights = [rootmean_gain, columns, *own, join(0), join(1)]
    own_rows = pending_microgroups[0]
    other_rows = swapped(own_rows, "expert", 1)
    pairs = [(e * legs, (e ^ 2) * legs) for e in range(places)]
    fresh_other = lax.ppermute(arriving_microgroups[1], ("expert", "section"), pairs)

    after = [own_rows]

    def stage(body, half, inputs, outs):
        operands = [table, *inputs, *weights]
        got = pl.pallas_call(
            body if half is None else functools.partial(body, half),
            out_shape=[rows_of(count) for count in outs],
            in_specs=[*[in_vmem] * len(operands), anywhere],
            out_specs=[in_vmem] * len(outs),
            compiler_params=pltpu.CompilerParams(vmem_limit_bytes=16 << 20),
        )(*operands, after[-1])
        after.append(got[0])
        return got

    def ahead(value, flip, wrap):
        last = legs if wrap else legs - 1
        perm = [
            (e * legs + s, (e ^ flip) * legs + (s + 1) % legs)
            for e in range(places)
            for s in range(last)
        ]
        return lax.ppermute(value, ("expert", "section"), perm)

    halves = (0, 1)
    inputs = [own_rows, other_rows, arriving_microgroups]
    both, *sent = stage(tick_0, None, inputs, (2 * num_rows, size, size))
    first = [ahead(sent[h], 2, True) for h in halves]
    straight = ahead(both, 0, True)
    done, second = [None] * 2, [None] * 2
    for h in halves:
        inputs = [straight, first[h], arriving_microgroups]
        done[h], sent = stage(tick_1_before, h, inputs, (size, size))
        second[h] = swapped(sent, "expert", 1)
    after_1, here = [None] * 2, [None] * 2
    for h in halves:
        inputs = [straight, done[h], arriving_microgroups, *first[: h + 1], *second[: h + 1]]
        outs = (2 * size, size, num_rows)[: h + 2]
        both, here[h], *was = stage(tick_1_after, h, inputs, outs)
        after_1[h] = ahead(both, 0, False)
    was = turned(was[0], "section", 1)
    third, back, last = [None] * 2, [None] * 2, [None] * 2
    for h in halves:
        (sent,) = stage(tick_2_before, h, [after_1[h], fresh_other], (size,))
        third[h] = swapped(sent, "expert", 1)
    for h in halves:
        back[h] = turned(third[h], "section", 1)
        (last[h],) = stage(tick_2_after, h, [after_1[h], third[h], arriving_microgroups], (size,))
    operands = [table, was, *[part for h in halves for part in (here[h], back[h], last[h])]]
    return pl.pallas_call(
        gather_kernel,
        out_shape=jax.ShapeDtypeStruct((1, TICKS, num_rows, width), jnp.bfloat16),
        in_specs=[in_vmem] * len(operands),
        out_specs=in_vmem,
        compiler_params=limited,
        name="gather",
    )(*operands)


def solution(mesh):
    placed = (
        P("section", ("groups", "expert"), None),
        P(None, ("groups", "expert"), None),
        P(None, "section", ("groups", "expert")),
        P("section", None),
        P("section", None, None),
        P("section", "expert", None, None),
        P("section", "expert", None, None),
    )

    paired = mesh.shape["expert"] == 4 and mesh.shape["groups"] == 2 and mesh.shape["section"] > 2

    def per_device(*args):
        if paired and args[4].shape[2] == 2 and args[5].shape[2] % 768 == 0:
            return pairs_per_device(*args)
        return slots_per_device(*args)

    return jax.shard_map(
        per_device,
        mesh=mesh,
        in_specs=placed,
        out_specs=P("section", None, ("groups", "expert"), None),
        check_vma=False,
    )
```

```python
import functools

import jax
import jax.numpy as jnp
from jax import lax
from jax.experimental import pallas as pl
from jax.experimental.pallas import tpu as pltpu
from jax.sharding import PartitionSpec as P


TICKS = 3


def swapped(x, axis, bit):
    return lax.ppermute(x, axis, [(i, i ^ 1 << bit) for i in range(lax.axis_size(axis))])


def from_behind(value, axis, steps):
    count = lax.axis_size(axis)
    initial, last = (max(0, -steps), min(count, count - steps))
    return lax.ppermute(value, axis, [(source, source + steps) for source in range(initial, last)])


def half_output(received, up_projection_matrix, down_projection_matrix):
    hidden = jnp.maximum(
        jnp.einsum(
            "sid,dh->sih", received, up_projection_matrix, preferred_element_type=jnp.float32
        ),
        0.0,
    ).astype(jnp.bfloat16)
    return jnp.einsum(
        "sih,hd->sid", hidden, down_projection_matrix, preferred_element_type=jnp.float32
    ).astype(jnp.bfloat16)


def expert_layer(
    tok_rows,
    routes,
    rootmean_gain,
    gating_columns,
    up_projection_matrix,
    down_projection_matrix,
    other_in,
    other_out,
):
    num_rows, width = tok_rows.shape
    experts = gating_columns.shape[1]
    capacity = min(num_rows, 3 * num_rows // experts)
    float_rows = tok_rows.astype(jnp.float32)
    inv_rms = lax.rsqrt(jnp.mean(float_rows * float_rows, axis=-1, keepdims=True) + 1e-06)
    normed = (float_rows * inv_rms * rootmean_gain).astype(jnp.bfloat16)
    logits = jnp.dot(normed, gating_columns, preferred_element_type=jnp.float32)
    one_hot = routes[:, None] == jnp.arange(experts, dtype=jnp.int32)[None, :]
    gate_value = jax.nn.sigmoid(jnp.sum(jnp.where(one_hot, logits, 0.0), axis=1))
    flags = one_hot.astype(jnp.int32)
    slot_rank = jnp.sum((jnp.cumsum(flags, axis=0) - flags) * flags, axis=1)
    slot_index = routes * capacity + slot_rank
    placing = (
        slot_index[None, :] == jnp.arange(experts * capacity, dtype=jnp.int32)[:, None]
    ).astype(jnp.bfloat16)
    outgoing = jnp.dot(placing, normed, preferred_element_type=jnp.float32).astype(jnp.bfloat16)
    outgoing = outgoing.reshape(experts, capacity, width)
    halves = outgoing.reshape(2 * experts, capacity // 2, width)
    received = lax.all_to_all(halves, "expert", split_axis=0, concat_axis=0, tiled=True)
    own_part = half_output(received, up_projection_matrix, down_projection_matrix)
    other_part = half_output(received, other_in, other_out)
    summed = (own_part.astype(jnp.float32) + other_part.astype(jnp.float32)).astype(jnp.bfloat16)
    combined = lax.all_to_all(summed, "expert", split_axis=0, concat_axis=0, tiled=True)
    flat_out = combined.reshape(experts * capacity, width)
    expert_out = lax.dot_general(
        placing, flat_out, (((0,), (0,)), ((), ())), preferred_element_type=jnp.float32
    )
    return (float_rows + gate_value[:, None] * expert_out).astype(jnp.bfloat16)


def slots_per_device(
    pending_microgroups,
    arriving_microgroups,
    expert_choice_grid,
    rootmean_gain,
    gating_columns,
    up_projection_matrix,
    down_projection_matrix,
):
    leg_position = lax.axis_index("section")
    own_in = up_projection_matrix[0, 0]
    own_out = down_projection_matrix[0, 0]
    other_in, other_out = swapped((own_in, own_out), "expert", 0)
    running_activation = pending_microgroups[0]
    per_tick = []
    for tick_idx in range(TICKS):
        layer_out = expert_layer(
            running_activation,
            expert_choice_grid[tick_idx, 0],
            rootmean_gain[0],
            gating_columns[0],
            own_in,
            own_out,
            other_in,
            other_out,
        )
        per_tick.append(layer_out)
        if tick_idx + 1 < TICKS:
            moved = from_behind(layer_out, "section", 1)
            running_activation = jnp.where(leg_position == 0, arriving_microgroups[tick_idx], moved)
    return jnp.stack(per_tick)[None]


def piece_list(width):
    direct = width // 4
    pieces = []
    for m, share in ((0, width // 2), (1, (width - direct) // 2)):
        pieces += [(m, r * (share // 3), share // 3, share) for r in range(3)]
    return [*pieces, (1, width - direct, direct, 0)]


def cut_kernel(some, *refs):
    count = len(some)
    sources, outs, sems = refs[: -count - 1], refs[-count - 1 : -1], refs[-1]
    group = lax.axis_index("groups")
    copies = []
    for index, ((m, first, size, share), out) in enumerate(zip(some, outs)):
        rows = pl.ds(pl.multiple_of(group * share + first, 16), size)
        copies.append(pltpu.make_async_copy(sources[m].at[rows, :], out, sems.at[index]))
    for copy in copies:
        copy.start()
    for copy in copies:
        copy.wait()


def join_kernel(some, *refs):
    refs, out_ref = list(refs[:-1]), refs[-1]
    group = lax.axis_index("groups")
    for _, first, size, share in some:
        for part in (group, 1 - group) if share else (0,):
            rows = pl.ds(pl.multiple_of(part * share + first, 16), size)
            out_ref[rows, :] = refs.pop(0)[...]


def mask_kernel(routes_ref, *refs):
    mask_ref = refs[-1]
    side = lax.axis_index("expert") // 2
    for tick in range(TICKS):
        serves = (routes_ref[tick, 0, 0] == side).astype(jnp.int32)
        mask_ref[tick : tick + 1] = jnp.full((1, mask_ref.shape[1]), serves, jnp.int32)


def layer_kernel(tick, which, last_tick, *refs):
    refs = list(refs)
    take = refs.pop
    mask_ref, straight_ref = take(0), take(0)
    cross_ref = take(0) if tick else None
    fresh_ref = take(0) if which == 0 else None
    gain_ref, columns_ref, up_ref, down_ref, far_up_ref, far_down_ref, _ = refs[:7]
    outs = refs[7:]
    leg = lax.axis_index("section")
    x = straight_ref[...].astype(jnp.float32)
    if tick:
        x = x + cross_ref[...].astype(jnp.float32)
        if which == 0:
            outs[1][...] = x.astype(jnp.bfloat16)
            x = jnp.where(leg == 0, fresh_ref[tick - 1].astype(jnp.float32), x)
    inv_rms = lax.rsqrt(jnp.mean(x * x, axis=-1, keepdims=True) + 1e-06)
    normed = (x * inv_rms * gain_ref[...]).astype(jnp.bfloat16)
    columns = columns_ref[...].astype(jnp.float32)
    column = jnp.where(lax.axis_index("expert") // 2 == 0, columns[0:1], columns[1:2])
    logit = jnp.sum(normed.astype(jnp.float32) * column, axis=-1, keepdims=True)
    hidden = []
    for ref in (up_ref, far_up_ref):
        up = jnp.dot(normed, ref[...], preferred_element_type=jnp.float32)
        hidden.append(jnp.maximum(up, 0.0).astype(jnp.bfloat16))
    out = jnp.dot(hidden[0], down_ref[...], preferred_element_type=jnp.float32)
    out = out + jnp.dot(hidden[1], far_down_ref[...], preferred_element_type=jnp.float32)
    y = x + jax.nn.sigmoid(logit) * out
    y = jnp.where(mask_ref[tick : tick + 1, :1] != 0, y, 0.0).astype(jnp.bfloat16)
    outs[0][...] = y
    if which == 0 and tick < last_tick:
        outs[-1][...] = jnp.where(leg == lax.axis_size("section") - 1, fresh_ref[tick], y)


def gather_kernel(first_ref, second_ref, own_ref, returned_ref, out_ref):
    out_ref[0, 0] = first_ref[...]
    out_ref[0, 1] = second_ref[...]
    total = own_ref[...].astype(jnp.float32) + returned_ref[...].astype(jnp.float32)
    out_ref[0, 2] = total.astype(jnp.bfloat16)


def pairs_per_device(
    pending_microgroups,
    arriving_microgroups,
    expert_choice_grid,
    rootmean_gain,
    gating_columns,
    up_projection_matrix,
    down_projection_matrix,
):
    places = lax.axis_size("expert")
    legs = lax.axis_size("section")
    own = (up_projection_matrix[0, 0], down_projection_matrix[0, 0])
    width, hid = own[0].shape
    num_rows = pending_microgroups.shape[1]
    pieces = piece_list(width)
    in_vmem = pl.BlockSpec(memory_space=pltpu.VMEM)
    anywhere = pl.BlockSpec(memory_space=pl.ANY)
    limited = pltpu.CompilerParams(vmem_limit_bytes=8 << 20)

    def cut(some):
        return pl.pallas_call(
            functools.partial(cut_kernel, some),
            out_shape=[jax.ShapeDtypeStruct((p[2], hid), jnp.bfloat16) for p in some],
            in_specs=[anywhere] * 2,
            out_specs=[in_vmem] * len(some),
            scratch_shapes=[pltpu.SemaphoreType.DMA((len(some),))],
            compiler_params=pltpu.CompilerParams(vmem_limit_bytes=60 << 20),
        )(*own)

    sending = [*cut(pieces[:1]), *cut(pieces[1:])]
    near, parts = [], {}
    for piece in sending:
        near.append(swapped(piece, "expert", 0))
    for index, piece in enumerate(near):
        parts[index] = [piece]
        if pieces[index][3]:
            parts[index].append(swapped(piece, "groups", 0))

    def join(m):
        chosen = [i for i, p in enumerate(pieces) if p[0] == m]
        operands = [part for i in chosen for part in parts[i]]
        return pl.pallas_call(
            functools.partial(join_kernel, [pieces[i] for i in chosen]),
            out_shape=jax.ShapeDtypeStruct((width, hid), jnp.bfloat16),
            in_specs=[in_vmem] * len(operands),
            out_specs=in_vmem,
            compiler_params=limited,
        )(*operands)

    columns = jnp.swapaxes(gating_columns[0], 0, 1)
    mask = pl.pallas_call(
        mask_kernel,
        out_shape=jax.ShapeDtypeStruct((8, 128), jnp.int32),
        in_specs=[pl.BlockSpec(memory_space=pltpu.SMEM)] + [in_vmem] * 5,
        out_specs=in_vmem,
        compiler_params=limited,
        name="mask",
    )(expert_choice_grid, *own, rootmean_gain, columns, arriving_microgroups)
    weights = [rootmean_gain, columns, *own, join(0), join(1)]
    own_rows = pending_microgroups[0]
    other_rows = swapped(own_rows, "expert", 1)
    rows_shape = jax.ShapeDtypeStruct((num_rows, width), jnp.bfloat16)

    def layer(tick, which, inputs, after):
        operands = [mask, *inputs]
        if which == 0:
            operands.append(arriving_microgroups)
        operands += weights
        extras = (which == 0) * ((tick > 0) + (tick + 1 < TICKS))
        return pl.pallas_call(
            functools.partial(layer_kernel, tick, which, TICKS - 1),
            out_shape=[rows_shape] * (1 + extras),
            in_specs=[*[in_vmem] * len(operands), anywhere],
            out_specs=[in_vmem] * (1 + extras),
            compiler_params=pltpu.CompilerParams(vmem_limit_bytes=16 << 20),
        )(*operands, after)

    def ahead(value, flip, wrap):
        last = legs if wrap else legs - 1
        perm = [
            (e * legs + s, (e ^ flip) * legs + (s + 1) % legs)
            for e in range(places)
            for s in range(last)
        ]
        return lax.ppermute(value, ("expert", "section"), perm)

    def back(value):
        return lax.ppermute(value, "section", [((s + 1) % legs, s) for s in range(legs)])

    current = {0: (own_rows,), 1: (other_rows,)}
    outputs = []
    after = own_rows
    for tick in range(TICKS):
        following = {}
        straight = {}
        done = {}
        for which in chunk_order(tick):
            got = layer(tick, which, current[which], after)
            after = done[which] = got[0]
            if tick + 1 < TICKS:
                following[1 - which] = ahead(got[-1], 2, True)
                straight[which] = ahead(got[0], 0, which == 0)
            elif which == 1:
                returned = swapped(got[0], "expert", 1)
            if tick and which == 0:
                outputs.append(back(got[1]))
        if tick + 1 < TICKS:
            current = {w: (straight[w], following[w]) for w in (0, 1)}
    return pl.pallas_call(
        gather_kernel,
        out_shape=jax.ShapeDtypeStruct((1, TICKS, num_rows, width), jnp.bfloat16),
        in_specs=[in_vmem] * 4,
        out_specs=in_vmem,
        compiler_params=limited,
        name="gather",
    )(*outputs, done[0], returned)


def chunk_order(tick):
    return (1, 0) if (TICKS - 1 - tick) % 2 == 0 else (0, 1)


def solution(mesh):
    placed = (
        P("section", ("groups", "expert"), None),
        P(None, ("groups", "expert"), None),
        P(None, "section", ("groups", "expert")),
        P("section", None),
        P("section", None, None),
        P("section", "expert", None, None),
        P("section", "expert", None, None),
    )

    paired = mesh.shape["expert"] == 4 and mesh.shape["groups"] == 2

    def per_device(*args):
        if paired and args[4].shape[2] == 2 and args[5].shape[2] % 768 == 0:
            return pairs_per_device(*args)
        return slots_per_device(*args)

    return jax.shard_map(
        per_device,
        mesh=mesh,
        in_specs=placed,
        out_specs=P("section", None, ("groups", "expert"), None),
        check_vma=False,
    )
```

```python
import functools

import jax
import jax.numpy as jnp
from jax import lax
from jax.experimental import pallas as pl
from jax.experimental.pallas import tpu as pltpu
from jax.sharding import PartitionSpec as P


TICKS = 3


def swapped(x, axis, bit):
    return lax.ppermute(x, axis, [(i, i ^ 1 << bit) for i in range(lax.axis_size(axis))])


def from_behind(value, axis, steps):
    count = lax.axis_size(axis)
    initial, last = (max(0, -steps), min(count, count - steps))
    return lax.ppermute(value, axis, [(source, source + steps) for source in range(initial, last)])


def half_output(received, up_projection_matrix, down_projection_matrix):
    hidden = jnp.maximum(
        jnp.einsum(
            "sid,dh->sih", received, up_projection_matrix, preferred_element_type=jnp.float32
        ),
        0.0,
    ).astype(jnp.bfloat16)
    return jnp.einsum(
        "sih,hd->sid", hidden, down_projection_matrix, preferred_element_type=jnp.float32
    ).astype(jnp.bfloat16)


def expert_layer(
    tok_rows,
    routes,
    rootmean_gain,
    gating_columns,
    up_projection_matrix,
    down_projection_matrix,
    other_in,
    other_out,
):
    num_rows, width = tok_rows.shape
    experts = gating_columns.shape[1]
    capacity = min(num_rows, 3 * num_rows // experts)
    float_rows = tok_rows.astype(jnp.float32)
    inv_rms = lax.rsqrt(jnp.mean(float_rows * float_rows, axis=-1, keepdims=True) + 1e-06)
    normed = (float_rows * inv_rms * rootmean_gain).astype(jnp.bfloat16)
    logits = jnp.dot(normed, gating_columns, preferred_element_type=jnp.float32)
    one_hot = routes[:, None] == jnp.arange(experts, dtype=jnp.int32)[None, :]
    gate_value = jax.nn.sigmoid(jnp.sum(jnp.where(one_hot, logits, 0.0), axis=1))
    flags = one_hot.astype(jnp.int32)
    slot_rank = jnp.sum((jnp.cumsum(flags, axis=0) - flags) * flags, axis=1)
    slot_index = routes * capacity + slot_rank
    placing = (
        slot_index[None, :] == jnp.arange(experts * capacity, dtype=jnp.int32)[:, None]
    ).astype(jnp.bfloat16)
    outgoing = jnp.dot(placing, normed, preferred_element_type=jnp.float32).astype(jnp.bfloat16)
    outgoing = outgoing.reshape(experts, capacity, width)
    halves = outgoing.reshape(2 * experts, capacity // 2, width)
    received = lax.all_to_all(halves, "expert", split_axis=0, concat_axis=0, tiled=True)
    own_part = half_output(received, up_projection_matrix, down_projection_matrix)
    other_part = half_output(received, other_in, other_out)
    summed = (own_part.astype(jnp.float32) + other_part.astype(jnp.float32)).astype(jnp.bfloat16)
    combined = lax.all_to_all(summed, "expert", split_axis=0, concat_axis=0, tiled=True)
    flat_out = combined.reshape(experts * capacity, width)
    expert_out = lax.dot_general(
        placing, flat_out, (((0,), (0,)), ((), ())), preferred_element_type=jnp.float32
    )
    return (float_rows + gate_value[:, None] * expert_out).astype(jnp.bfloat16)


def slots_per_device(
    pending_microgroups,
    arriving_microgroups,
    expert_choice_grid,
    rootmean_gain,
    gating_columns,
    up_projection_matrix,
    down_projection_matrix,
):
    leg_position = lax.axis_index("section")
    own_in = up_projection_matrix[0, 0]
    own_out = down_projection_matrix[0, 0]
    other_in, other_out = swapped((own_in, own_out), "expert", 0)
    running_activation = pending_microgroups[0]
    per_tick = []
    for tick_idx in range(TICKS):
        layer_out = expert_layer(
            running_activation,
            expert_choice_grid[tick_idx, 0],
            rootmean_gain[0],
            gating_columns[0],
            own_in,
            own_out,
            other_in,
            other_out,
        )
        per_tick.append(layer_out)
        if tick_idx + 1 < TICKS:
            moved = from_behind(layer_out, "section", 1)
            running_activation = jnp.where(leg_position == 0, arriving_microgroups[tick_idx], moved)
    return jnp.stack(per_tick)[None]


def piece_list(width):
    direct = width // 8
    pieces = []
    for m, share in ((0, width // 2), (1, (width - direct) // 2)):
        pieces += [(m, r * (share // 3), share // 3, share) for r in range(3)]
    return [*pieces, (1, width - direct, direct, 0)]


def cut_kernel(some, *refs):
    count = len(some)
    sources, outs, sems = refs[: -count - 1], refs[-count - 1 : -1], refs[-1]
    group = lax.axis_index("groups")
    copies = []
    for index, ((m, first, size, share), out) in enumerate(zip(some, outs)):
        rows = pl.ds(pl.multiple_of(group * share + first, 16), size)
        copies.append(pltpu.make_async_copy(sources[m].at[rows, :], out, sems.at[index]))
    for copy in copies:
        copy.start()
    for copy in copies:
        copy.wait()


def join_kernel(some, *refs):
    refs, out_ref = list(refs[:-1]), refs[-1]
    group = lax.axis_index("groups")
    for _, first, size, share in some:
        for part in (group, 1 - group) if share else (0,):
            rows = pl.ds(pl.multiple_of(part * share + first, 16), size)
            out_ref[rows, :] = refs.pop(0)[...]


def mask_kernel(routes_ref, *refs):
    mask_ref = refs[-1]
    side = lax.axis_index("expert") // 2
    for tick in range(TICKS):
        serves = (routes_ref[tick, 0, 0] == side).astype(jnp.int32)
        mask_ref[tick : tick + 1] = jnp.full((1, mask_ref.shape[1]), serves, jnp.int32)


def layer_kernel(tick, which, last_tick, *refs):
    refs = list(refs)
    take = refs.pop
    mask_ref, straight_ref = take(0), take(0)
    cross_ref = take(0) if tick or which else None
    fresh_ref = take(0) if which == 0 else None
    gain_ref, columns_ref, up_ref, down_ref, far_up_ref, far_down_ref, _ = refs[:7]
    outs = refs[7:]
    leg = lax.axis_index("section")
    x = straight_ref[...].astype(jnp.float32)
    if tick or which:
        x = x + cross_ref[...].astype(jnp.float32)
        if which == 0:
            outs[1][...] = x.astype(jnp.bfloat16)
            x = jnp.where(leg == 0, fresh_ref[tick - 1].astype(jnp.float32), x)
    inv_rms = lax.rsqrt(jnp.mean(x * x, axis=-1, keepdims=True) + 1e-06)
    normed = (x * inv_rms * gain_ref[...]).astype(jnp.bfloat16)
    columns = columns_ref[...].astype(jnp.float32)
    column = jnp.where(lax.axis_index("expert") // 2 == 0, columns[0:1], columns[1:2])
    logit = jnp.sum(normed.astype(jnp.float32) * column, axis=-1, keepdims=True)
    hidden = []
    for ref in (up_ref, far_up_ref):
        up = jnp.dot(normed, ref[...], preferred_element_type=jnp.float32)
        hidden.append(jnp.maximum(up, 0.0).astype(jnp.bfloat16))
    out = jnp.dot(hidden[0], down_ref[...], preferred_element_type=jnp.float32)
    out = out + jnp.dot(hidden[1], far_down_ref[...], preferred_element_type=jnp.float32)
    y = x + jax.nn.sigmoid(logit) * out
    y = jnp.where(mask_ref[tick : tick + 1, :1] != 0, y, 0.0).astype(jnp.bfloat16)
    outs[0][...] = y
    if which == 0 and tick < last_tick:
        outs[-1][...] = jnp.where(leg == lax.axis_size("section") - 1, fresh_ref[tick], y)


def gather_kernel(first_ref, second_ref, own_ref, returned_ref, out_ref):
    out_ref[0, 0] = first_ref[...]
    out_ref[0, 1] = second_ref[...]
    total = own_ref[...].astype(jnp.float32) + returned_ref[...].astype(jnp.float32)
    out_ref[0, 2] = total.astype(jnp.bfloat16)


def pairs_per_device(
    pending_microgroups,
    arriving_microgroups,
    expert_choice_grid,
    rootmean_gain,
    gating_columns,
    up_projection_matrix,
    down_projection_matrix,
):
    places = lax.axis_size("expert")
    legs = lax.axis_size("section")
    own = (up_projection_matrix[0, 0], down_projection_matrix[0, 0])
    width, hid = own[0].shape
    num_rows = pending_microgroups.shape[1]
    pieces = piece_list(width)
    in_vmem = pl.BlockSpec(memory_space=pltpu.VMEM)
    anywhere = pl.BlockSpec(memory_space=pl.ANY)
    limited = pltpu.CompilerParams(vmem_limit_bytes=8 << 20)

    def cut(some):
        return pl.pallas_call(
            functools.partial(cut_kernel, some),
            out_shape=[pltpu.VMEM((p[2], hid), jnp.bfloat16) for p in some],
            in_specs=[anywhere] * 2,
            out_specs=[in_vmem] * len(some),
            scratch_shapes=[pltpu.SemaphoreType.DMA((len(some),))],
            compiler_params=pltpu.CompilerParams(vmem_limit_bytes=58 << 20),
        )(*own)

    sending = [*cut(pieces[:1]), *cut(pieces[1:])]
    near, parts = [], {}
    for piece in sending:
        near.append(swapped(piece, "expert", 0))
    for index, piece in enumerate(near):
        parts[index] = [piece]
        if pieces[index][3]:
            parts[index].append(swapped(piece, "groups", 0))

    def join(m):
        chosen = [i for i, p in enumerate(pieces) if p[0] == m]
        operands = [part for i in chosen for part in parts[i]]
        return pl.pallas_call(
            functools.partial(join_kernel, [pieces[i] for i in chosen]),
            out_shape=jax.ShapeDtypeStruct((width, hid), jnp.bfloat16),
            in_specs=[in_vmem] * len(operands),
            out_specs=in_vmem,
            compiler_params=limited,
        )(*operands)

    columns = jnp.swapaxes(gating_columns[0], 0, 1)
    mask = pl.pallas_call(
        mask_kernel,
        out_shape=jax.ShapeDtypeStruct((8, 128), jnp.int32),
        in_specs=[pl.BlockSpec(memory_space=pltpu.SMEM)] + [in_vmem] * 5,
        out_specs=in_vmem,
        compiler_params=limited,
        name="mask",
    )(expert_choice_grid, *own, rootmean_gain, columns, arriving_microgroups)
    weights = [rootmean_gain, columns, *own, join(0), join(1)]
    own_rows = pending_microgroups[0]
    other_rows = []
    for senders in ((0, places - 1), range(1, places - 1)):
        other_rows.append(lax.ppermute(own_rows, "expert", [(e, e ^ 2) for e in senders]))
    rows_shape = jax.ShapeDtypeStruct((num_rows, width), jnp.bfloat16)

    def layer(tick, which, inputs, after):
        operands = [mask, *inputs]
        if which == 0:
            operands.append(arriving_microgroups)
        operands += weights
        extras = (which == 0) * ((tick > 0) + (tick + 1 < TICKS))
        return pl.pallas_call(
            functools.partial(layer_kernel, tick, which, TICKS - 1),
            out_shape=[rows_shape] * (1 + extras),
            in_specs=[*[in_vmem] * len(operands), anywhere],
            out_specs=[in_vmem] * (1 + extras),
            compiler_params=pltpu.CompilerParams(vmem_limit_bytes=16 << 20),
        )(*operands, after)

    def ahead(value, flip, wrap):
        last = legs if wrap else legs - 1
        perm = [
            (e * legs + s, (e ^ flip) * legs + (s + 1) % legs)
            for e in range(places)
            for s in range(last)
        ]
        return lax.ppermute(value, ("expert", "section"), perm)

    def back(value):
        return lax.ppermute(value, "section", [((s + 1) % legs, s) for s in range(legs)])

    current = {0: (own_rows,), 1: other_rows}
    outputs = []
    after = own_rows
    for tick in range(TICKS):
        following = {}
        straight = {}
        done = {}
        for which in chunk_order(tick):
            got = layer(tick, which, current[which], after)
            after = done[which] = got[0]
            if tick + 1 < TICKS:
                following[1 - which] = ahead(got[-1], 2, True)
                straight[which] = ahead(got[0], 0, which == 0)
            elif which == 1:
                returned = swapped(got[0], "expert", 1)
            if tick and which == 0:
                outputs.append(back(got[1]))
        if tick + 1 < TICKS:
            current = {w: (straight[w], following[w]) for w in (0, 1)}
    return pl.pallas_call(
        gather_kernel,
        out_shape=jax.ShapeDtypeStruct((1, TICKS, num_rows, width), jnp.bfloat16),
        in_specs=[in_vmem] * 4,
        out_specs=in_vmem,
        compiler_params=limited,
        name="gather",
    )(*outputs, done[0], returned)


def chunk_order(tick):
    return (1, 0) if (TICKS - 1 - tick) % 2 == 0 else (0, 1)


def solution(mesh):
    placed = (
        P("section", ("groups", "expert"), None),
        P(None, ("groups", "expert"), None),
        P(None, "section", ("groups", "expert")),
        P("section", None),
        P("section", None, None),
        P("section", "expert", None, None),
        P("section", "expert", None, None),
    )

    paired = mesh.shape["expert"] == 4 and mesh.shape["groups"] == 2

    def per_device(*args):
        if paired and args[4].shape[2] == 2 and args[5].shape[2] % 768 == 0:
            return pairs_per_device(*args)
        return slots_per_device(*args)

    return jax.shard_map(
        per_device,
        mesh=mesh,
        in_specs=placed,
        out_specs=P("section", None, ("groups", "expert"), None),
        check_vma=False,
    )
```

```python
import functools

import jax
import jax.numpy as jnp
from jax import lax
from jax.experimental import pallas as pl
from jax.experimental.pallas import tpu as pltpu
from jax.sharding import PartitionSpec as P


TICKS = 3


def swapped(x, axis, bit):
    return lax.ppermute(x, axis, [(i, i ^ 1 << bit) for i in range(lax.axis_size(axis))])


def from_behind(value, axis, steps):
    count = lax.axis_size(axis)
    initial, last = (max(0, -steps), min(count, count - steps))
    return lax.ppermute(value, axis, [(source, source + steps) for source in range(initial, last)])


def half_output(received, up_projection_matrix, down_projection_matrix):
    hidden = jnp.maximum(
        jnp.einsum(
            "sid,dh->sih", received, up_projection_matrix, preferred_element_type=jnp.float32
        ),
        0.0,
    ).astype(jnp.bfloat16)
    return jnp.einsum(
        "sih,hd->sid", hidden, down_projection_matrix, preferred_element_type=jnp.float32
    ).astype(jnp.bfloat16)


def expert_layer(
    tok_rows,
    routes,
    rootmean_gain,
    gating_columns,
    up_projection_matrix,
    down_projection_matrix,
    other_in,
    other_out,
):
    num_rows, width = tok_rows.shape
    experts = gating_columns.shape[1]
    capacity = min(num_rows, 3 * num_rows // experts)
    float_rows = tok_rows.astype(jnp.float32)
    inv_rms = lax.rsqrt(jnp.mean(float_rows * float_rows, axis=-1, keepdims=True) + 1e-06)
    normed = (float_rows * inv_rms * rootmean_gain).astype(jnp.bfloat16)
    logits = jnp.dot(normed, gating_columns, preferred_element_type=jnp.float32)
    one_hot = routes[:, None] == jnp.arange(experts, dtype=jnp.int32)[None, :]
    gate_value = jax.nn.sigmoid(jnp.sum(jnp.where(one_hot, logits, 0.0), axis=1))
    flags = one_hot.astype(jnp.int32)
    slot_rank = jnp.sum((jnp.cumsum(flags, axis=0) - flags) * flags, axis=1)
    slot_index = routes * capacity + slot_rank
    placing = (
        slot_index[None, :] == jnp.arange(experts * capacity, dtype=jnp.int32)[:, None]
    ).astype(jnp.bfloat16)
    outgoing = jnp.dot(placing, normed, preferred_element_type=jnp.float32).astype(jnp.bfloat16)
    outgoing = outgoing.reshape(experts, capacity, width)
    halves = outgoing.reshape(2 * experts, capacity // 2, width)
    received = lax.all_to_all(halves, "expert", split_axis=0, concat_axis=0, tiled=True)
    own_part = half_output(received, up_projection_matrix, down_projection_matrix)
    other_part = half_output(received, other_in, other_out)
    summed = (own_part.astype(jnp.float32) + other_part.astype(jnp.float32)).astype(jnp.bfloat16)
    combined = lax.all_to_all(summed, "expert", split_axis=0, concat_axis=0, tiled=True)
    flat_out = combined.reshape(experts * capacity, width)
    expert_out = lax.dot_general(
        placing, flat_out, (((0,), (0,)), ((), ())), preferred_element_type=jnp.float32
    )
    return (float_rows + gate_value[:, None] * expert_out).astype(jnp.bfloat16)


def slots_per_device(
    pending_microgroups,
    arriving_microgroups,
    expert_choice_grid,
    rootmean_gain,
    gating_columns,
    up_projection_matrix,
    down_projection_matrix,
):
    leg_position = lax.axis_index("section")
    own_in = up_projection_matrix[0, 0]
    own_out = down_projection_matrix[0, 0]
    other_in, other_out = swapped((own_in, own_out), "expert", 0)
    running_activation = pending_microgroups[0]
    per_tick = []
    for tick_idx in range(TICKS):
        layer_out = expert_layer(
            running_activation,
            expert_choice_grid[tick_idx, 0],
            rootmean_gain[0],
            gating_columns[0],
            own_in,
            own_out,
            other_in,
            other_out,
        )
        per_tick.append(layer_out)
        if tick_idx + 1 < TICKS:
            moved = from_behind(layer_out, "section", 1)
            running_activation = jnp.where(leg_position == 0, arriving_microgroups[tick_idx], moved)
    return jnp.stack(per_tick)[None]


def piece_list(width):
    direct = width // 8
    pieces = []
    for m, share in ((0, width // 2), (1, (width - direct) // 2)):
        pieces += [(m, r * (share // 3), share // 3, share) for r in range(3)]
    return [*pieces, (1, width - direct, direct, 0)]


def cut_kernel(some, *refs):
    count = len(some)
    sources, outs, sems = refs[: -count - 1], refs[-count - 1 : -1], refs[-1]
    group = lax.axis_index("groups")
    copies = []
    for index, ((m, first, size, share), out) in enumerate(zip(some, outs)):
        rows = pl.ds(pl.multiple_of(group * share + first, 16), size)
        copies.append(pltpu.make_async_copy(sources[m].at[rows, :], out, sems.at[index]))
    for copy in copies:
        copy.start()
    for copy in copies:
        copy.wait()


def join_kernel(some, *refs):
    refs, out_ref = list(refs[:-1]), refs[-1]
    group = lax.axis_index("groups")
    for _, first, size, share in some:
        for part in (group, 1 - group) if share else (0,):
            rows = pl.ds(pl.multiple_of(part * share + first, 16), size)
            out_ref[rows, :] = refs.pop(0)[...]


def mask_kernel(routes_ref, *refs):
    mask_ref = refs[-1]
    side = lax.axis_index("expert") // 2
    for tick in range(TICKS):
        serves = (routes_ref[tick, 0, 0] == side).astype(jnp.int32)
        mask_ref[tick : tick + 1] = jnp.full((1, mask_ref.shape[1]), serves, jnp.int32)


def layer_kernel(tick, which, last_tick, *refs):
    refs = list(refs)
    take = refs.pop
    mask_ref, straight_ref = take(0), take(0)
    cross_ref = take(0) if tick or which else None
    fresh_ref = take(0) if which == 0 else None
    gain_ref, columns_ref, up_ref, down_ref, far_up_ref, far_down_ref, _ = refs[:7]
    outs = refs[7:]
    leg = lax.axis_index("section")
    x = straight_ref[...].astype(jnp.float32)
    if tick or which:
        x = x + cross_ref[...].astype(jnp.float32)
        if which == 0:
            outs[1][...] = x.astype(jnp.bfloat16)
            x = jnp.where(leg == 0, fresh_ref[tick - 1].astype(jnp.float32), x)
    sent = outs[-1] if which == 0 and tick < last_tick else None

    def give(y):
        outs[0][...] = y
        if sent is not None:
            sent[...] = jnp.where(leg == lax.axis_size("section") - 1, fresh_ref[tick], y)

    serves = jnp.max(mask_ref[tick : tick + 1, :]) != 0

    @pl.when(serves)
    def _():
        inv_rms = lax.rsqrt(jnp.mean(x * x, axis=-1, keepdims=True) + 1e-06)
        normed = (x * inv_rms * gain_ref[...]).astype(jnp.bfloat16)
        columns = columns_ref[...].astype(jnp.float32)
        column = jnp.where(lax.axis_index("expert") // 2 == 0, columns[0:1], columns[1:2])
        logit = jnp.sum(normed.astype(jnp.float32) * column, axis=-1, keepdims=True)
        hidden = []
        for ref in (up_ref, far_up_ref):
            up = jnp.dot(normed, ref[...], preferred_element_type=jnp.float32)
            hidden.append(jnp.maximum(up, 0.0).astype(jnp.bfloat16))
        out = jnp.dot(hidden[0], down_ref[...], preferred_element_type=jnp.float32)
        out = out + jnp.dot(hidden[1], far_down_ref[...], preferred_element_type=jnp.float32)
        give((x + jax.nn.sigmoid(logit) * out).astype(jnp.bfloat16))

    @pl.when(jnp.logical_not(serves))
    def _():
        give(jnp.zeros(x.shape, jnp.bfloat16))


def gather_kernel(first_ref, second_ref, own_ref, returned_ref, out_ref):
    out_ref[0, 0] = first_ref[...]
    out_ref[0, 1] = second_ref[...]
    total = own_ref[...].astype(jnp.float32) + returned_ref[...].astype(jnp.float32)
    out_ref[0, 2] = total.astype(jnp.bfloat16)


def pairs_per_device(
    pending_microgroups,
    arriving_microgroups,
    expert_choice_grid,
    rootmean_gain,
    gating_columns,
    up_projection_matrix,
    down_projection_matrix,
):
    places = lax.axis_size("expert")
    legs = lax.axis_size("section")
    own = (up_projection_matrix[0, 0], down_projection_matrix[0, 0])
    width, hid = own[0].shape
    num_rows = pending_microgroups.shape[1]
    pieces = piece_list(width)
    in_vmem = pl.BlockSpec(memory_space=pltpu.VMEM)
    anywhere = pl.BlockSpec(memory_space=pl.ANY)
    limited = pltpu.CompilerParams(vmem_limit_bytes=8 << 20)

    def cut(some):
        return pl.pallas_call(
            functools.partial(cut_kernel, some),
            out_shape=[pltpu.VMEM((p[2], hid), jnp.bfloat16) for p in some],
            in_specs=[anywhere] * 2,
            out_specs=[in_vmem] * len(some),
            scratch_shapes=[pltpu.SemaphoreType.DMA((len(some),))],
            compiler_params=pltpu.CompilerParams(vmem_limit_bytes=58 << 20),
        )(*own)

    sending = [*cut(pieces[:1]), *cut(pieces[1:])]
    near, parts = [], {}
    for piece in sending:
        near.append(swapped(piece, "expert", 0))
    for index, piece in enumerate(near):
        parts[index] = [piece]
        if pieces[index][3]:
            parts[index].append(swapped(piece, "groups", 0))

    def join(m):
        chosen = [i for i, p in enumerate(pieces) if p[0] == m]
        operands = [part for i in chosen for part in parts[i]]
        return pl.pallas_call(
            functools.partial(join_kernel, [pieces[i] for i in chosen]),
            out_shape=jax.ShapeDtypeStruct((width, hid), jnp.bfloat16),
            in_specs=[in_vmem] * len(operands),
            out_specs=in_vmem,
            compiler_params=limited,
        )(*operands)

    columns = jnp.swapaxes(gating_columns[0], 0, 1)
    mask = pl.pallas_call(
        mask_kernel,
        out_shape=jax.ShapeDtypeStruct((8, 128), jnp.int32),
        in_specs=[pl.BlockSpec(memory_space=pltpu.SMEM)] + [in_vmem] * 5,
        out_specs=in_vmem,
        compiler_params=limited,
        name="mask",
    )(expert_choice_grid, *own, rootmean_gain, columns, arriving_microgroups)
    weights = [rootmean_gain, columns, *own, join(0), join(1)]
    own_rows = pending_microgroups[0]
    other_rows = []
    for senders in ((0, places - 1), range(1, places - 1)):
        other_rows.append(lax.ppermute(own_rows, "expert", [(e, places - 1 - e) for e in senders]))
    rows_shape = jax.ShapeDtypeStruct((num_rows, width), jnp.bfloat16)

    def layer(tick, which, inputs, after):
        operands = [mask, *inputs]
        if which == 0:
            operands.append(arriving_microgroups)
        operands += weights
        extras = (which == 0) * ((tick > 0) + (tick + 1 < TICKS))
        return pl.pallas_call(
            functools.partial(layer_kernel, tick, which, TICKS - 1),
            out_shape=[rows_shape] * (1 + extras),
            in_specs=[*[in_vmem] * len(operands), anywhere],
            out_specs=[in_vmem] * (1 + extras),
            compiler_params=pltpu.CompilerParams(vmem_limit_bytes=16 << 20),
        )(*operands, after)

    def ahead(value, flip, wrap):
        last = legs if wrap else legs - 1
        perm = [
            (e * legs + s, (places - 1 - e if flip else e) * legs + (s + 1) % legs)
            for e in range(places)
            for s in range(last)
        ]
        return lax.ppermute(value, ("expert", "section"), perm)

    def back(value):
        return lax.ppermute(value, "section", [((s + 1) % legs, s) for s in range(legs)])

    current = {0: (own_rows,), 1: other_rows}
    outputs = []
    after = own_rows
    for tick in range(TICKS):
        following = {}
        straight = {}
        done = {}
        for which in chunk_order(tick):
            got = layer(tick, which, current[which], after)
            after = done[which] = got[0]
            if tick + 1 < TICKS:
                following[1 - which] = ahead(got[-1], True, True)
                straight[which] = ahead(got[0], False, which == 0)
            elif which == 1:
                mirror = [(e, places - 1 - e) for e in range(places)]
                returned = lax.ppermute(got[0], "expert", mirror)
            if tick and which == 0:
                outputs.append(back(got[1]))
        if tick + 1 < TICKS:
            current = {w: (straight[w], following[w]) for w in (0, 1)}
    return pl.pallas_call(
        gather_kernel,
        out_shape=jax.ShapeDtypeStruct((1, TICKS, num_rows, width), jnp.bfloat16),
        in_specs=[in_vmem] * 4,
        out_specs=in_vmem,
        compiler_params=limited,
        name="gather",
    )(*outputs, done[0], returned)


def chunk_order(tick):
    return (1, 0) if (TICKS - 1 - tick) % 2 == 0 else (0, 1)


def solution(mesh):
    placed = (
        P("section", ("groups", "expert"), None),
        P(None, ("groups", "expert"), None),
        P(None, "section", ("groups", "expert")),
        P("section", None),
        P("section", None, None),
        P("section", "expert", None, None),
        P("section", "expert", None, None),
    )

    paired = mesh.shape["expert"] == 4 and mesh.shape["groups"] == 2

    def per_device(*args):
        if paired and args[4].shape[2] == 2 and args[5].shape[2] % 768 == 0:
            return pairs_per_device(*args)
        return slots_per_device(*args)

    return jax.shard_map(
        per_device,
        mesh=mesh,
        in_specs=placed,
        out_specs=P("section", None, ("groups", "expert"), None),
        check_vma=False,
    )
```

```python
import functools

import jax
import jax.numpy as jnp
from jax import lax
from jax.experimental import pallas as pl
from jax.experimental.pallas import tpu as pltpu
from jax.sharding import PartitionSpec as P


TICKS = 3


def swapped(x, axis, bit):
    return lax.ppermute(x, axis, [(i, i ^ 1 << bit) for i in range(lax.axis_size(axis))])


def from_behind(value, axis, steps):
    count = lax.axis_size(axis)
    initial, last = (max(0, -steps), min(count, count - steps))
    return lax.ppermute(value, axis, [(source, source + steps) for source in range(initial, last)])


def half_output(received, up_projection_matrix, down_projection_matrix):
    hidden = jnp.maximum(
        jnp.einsum(
            "sid,dh->sih", received, up_projection_matrix, preferred_element_type=jnp.float32
        ),
        0.0,
    ).astype(jnp.bfloat16)
    return jnp.einsum(
        "sih,hd->sid", hidden, down_projection_matrix, preferred_element_type=jnp.float32
    ).astype(jnp.bfloat16)


def expert_layer(
    tok_rows,
    routes,
    rootmean_gain,
    gating_columns,
    up_projection_matrix,
    down_projection_matrix,
    other_in,
    other_out,
):
    num_rows, width = tok_rows.shape
    experts = gating_columns.shape[1]
    capacity = min(num_rows, 3 * num_rows // experts)
    float_rows = tok_rows.astype(jnp.float32)
    inv_rms = lax.rsqrt(jnp.mean(float_rows * float_rows, axis=-1, keepdims=True) + 1e-06)
    normed = (float_rows * inv_rms * rootmean_gain).astype(jnp.bfloat16)
    logits = jnp.dot(normed, gating_columns, preferred_element_type=jnp.float32)
    one_hot = routes[:, None] == jnp.arange(experts, dtype=jnp.int32)[None, :]
    gate_value = jax.nn.sigmoid(jnp.sum(jnp.where(one_hot, logits, 0.0), axis=1))
    flags = one_hot.astype(jnp.int32)
    slot_rank = jnp.sum((jnp.cumsum(flags, axis=0) - flags) * flags, axis=1)
    slot_index = routes * capacity + slot_rank
    placing = (
        slot_index[None, :] == jnp.arange(experts * capacity, dtype=jnp.int32)[:, None]
    ).astype(jnp.bfloat16)
    outgoing = jnp.dot(placing, normed, preferred_element_type=jnp.float32).astype(jnp.bfloat16)
    outgoing = outgoing.reshape(experts, capacity, width)
    halves = outgoing.reshape(2 * experts, capacity // 2, width)
    received = lax.all_to_all(halves, "expert", split_axis=0, concat_axis=0, tiled=True)
    own_part = half_output(received, up_projection_matrix, down_projection_matrix)
    other_part = half_output(received, other_in, other_out)
    summed = (own_part.astype(jnp.float32) + other_part.astype(jnp.float32)).astype(jnp.bfloat16)
    combined = lax.all_to_all(summed, "expert", split_axis=0, concat_axis=0, tiled=True)
    flat_out = combined.reshape(experts * capacity, width)
    expert_out = lax.dot_general(
        placing, flat_out, (((0,), (0,)), ((), ())), preferred_element_type=jnp.float32
    )
    return (float_rows + gate_value[:, None] * expert_out).astype(jnp.bfloat16)


def slots_per_device(
    pending_microgroups,
    arriving_microgroups,
    expert_choice_grid,
    rootmean_gain,
    gating_columns,
    up_projection_matrix,
    down_projection_matrix,
):
    leg_position = lax.axis_index("section")
    own_in = up_projection_matrix[0, 0]
    own_out = down_projection_matrix[0, 0]
    other_in, other_out = swapped((own_in, own_out), "expert", 0)
    running_activation = pending_microgroups[0]
    per_tick = []
    for tick_idx in range(TICKS):
        layer_out = expert_layer(
            running_activation,
            expert_choice_grid[tick_idx, 0],
            rootmean_gain[0],
            gating_columns[0],
            own_in,
            own_out,
            other_in,
            other_out,
        )
        per_tick.append(layer_out)
        if tick_idx + 1 < TICKS:
            moved = from_behind(layer_out, "section", 1)
            running_activation = jnp.where(leg_position == 0, arriving_microgroups[tick_idx], moved)
    return jnp.stack(per_tick)[None]


def piece_list(width):
    direct = width // 4
    pieces = []
    for m, share in ((0, width // 2), (1, (width - direct) // 2)):
        pieces += [(m, r * (share // 3), share // 3, share) for r in range(3)]
    return [*pieces, (1, width - direct, direct, 0)]


def cut_kernel(some, *refs):
    count = len(some)
    sources, outs, sems = refs[: -count - 1], refs[-count - 1 : -1], refs[-1]
    group = lax.axis_index("groups")
    copies = []
    for index, ((m, first, size, share), out) in enumerate(zip(some, outs)):
        rows = pl.ds(pl.multiple_of(group * share + first, 16), size)
        copies.append(pltpu.make_async_copy(sources[m].at[rows, :], out, sems.at[index]))
    for copy in copies:
        copy.start()
    for copy in copies:
        copy.wait()


def join_kernel(some, *refs):
    refs, out_ref = list(refs[:-1]), refs[-1]
    group = lax.axis_index("groups")
    for _, first, size, share in some:
        for part in (group, 1 - group) if share else (0,):
            rows = pl.ds(pl.multiple_of(part * share + first, 16), size)
            out_ref[rows, :] = refs.pop(0)[...]


def mask_kernel(routes_ref, *refs):
    mask_ref = refs[-1]
    side = lax.axis_index("expert") // 2
    for tick in range(TICKS):
        serves = (routes_ref[tick, 0, 0] == side).astype(jnp.int32)
        mask_ref[tick : tick + 1] = jnp.full((1, mask_ref.shape[1]), serves, jnp.int32)


def layer_kernel(tick, which, last_tick, *refs):
    refs = list(refs)
    take = refs.pop
    mask_ref, straight_ref = take(0), take(0)
    cross_ref = take(0) if tick or which else None
    fresh_ref = take(0) if which == 0 else None
    gain_ref, columns_ref, up_ref, down_ref, far_up_ref, far_down_ref, _ = refs[:7]
    outs = refs[7:]
    leg = lax.axis_index("section")
    x = straight_ref[...].astype(jnp.float32)
    if tick or which:
        x = x + cross_ref[...].astype(jnp.float32)
        if which == 0:
            outs[1][...] = x.astype(jnp.bfloat16)
            x = jnp.where(leg == 0, fresh_ref[tick - 1].astype(jnp.float32), x)
    sent = outs[-1] if which == 0 and tick < last_tick else None

    def give(y):
        outs[0][...] = y
        if sent is not None:
            sent[...] = jnp.where(leg == lax.axis_size("section") - 1, fresh_ref[tick], y)

    serves = jnp.max(mask_ref[tick : tick + 1, :]) != 0

    @pl.when(serves)
    def _():
        inv_rms = lax.rsqrt(jnp.mean(x * x, axis=-1, keepdims=True) + 1e-06)
        normed = (x * inv_rms * gain_ref[...]).astype(jnp.bfloat16)
        columns = columns_ref[...].astype(jnp.float32)
        column = jnp.where(lax.axis_index("expert") // 2 == 0, columns[0:1], columns[1:2])
        logit = jnp.sum(normed.astype(jnp.float32) * column, axis=-1, keepdims=True)
        hidden = []
        for ref in (up_ref, far_up_ref):
            up = jnp.dot(normed, ref[...], preferred_element_type=jnp.float32)
            hidden.append(jnp.maximum(up, 0.0).astype(jnp.bfloat16))
        out = jnp.dot(hidden[0], down_ref[...], preferred_element_type=jnp.float32)
        out = out + jnp.dot(hidden[1], far_down_ref[...], preferred_element_type=jnp.float32)
        give((x + jax.nn.sigmoid(logit) * out).astype(jnp.bfloat16))

    @pl.when(jnp.logical_not(serves))
    def _():
        give(jnp.zeros(x.shape, jnp.bfloat16))


def gather_kernel(first_ref, second_ref, own_ref, returned_ref, out_ref, last_ref, sems):
    rows = (first_ref, second_ref, last_ref)
    copies = [
        pltpu.make_async_copy(ref, out_ref.at[0, tick], sems.at[tick])
        for tick, ref in enumerate(rows)
    ]
    copies[0].start()
    copies[1].start()
    total = own_ref[...].astype(jnp.float32) + returned_ref[...].astype(jnp.float32)
    last_ref[...] = total.astype(jnp.bfloat16)
    copies[2].start()
    for copy in copies:
        copy.wait()


def pairs_per_device(
    pending_microgroups,
    arriving_microgroups,
    expert_choice_grid,
    rootmean_gain,
    gating_columns,
    up_projection_matrix,
    down_projection_matrix,
):
    places = lax.axis_size("expert")
    legs = lax.axis_size("section")
    own = (up_projection_matrix[0, 0], down_projection_matrix[0, 0])
    width, hid = own[0].shape
    num_rows = pending_microgroups.shape[1]
    pieces = piece_list(width)
    in_vmem = pl.BlockSpec(memory_space=pltpu.VMEM)
    anywhere = pl.BlockSpec(memory_space=pl.ANY)
    limited = pltpu.CompilerParams(vmem_limit_bytes=8 << 20)

    def cut(some):
        return pl.pallas_call(
            functools.partial(cut_kernel, some),
            out_shape=[pltpu.VMEM((p[2], hid), jnp.bfloat16) for p in some],
            in_specs=[anywhere] * 2,
            out_specs=[in_vmem] * len(some),
            scratch_shapes=[pltpu.SemaphoreType.DMA((len(some),))],
            compiler_params=pltpu.CompilerParams(vmem_limit_bytes=58 << 20),
        )(*own)

    sending = [*cut(pieces[:1]), *cut(pieces[1:])]
    near, parts = [], {}
    for piece in sending:
        near.append(swapped(piece, "expert", 0))
    for index, piece in enumerate(near):
        parts[index] = [piece]
        if pieces[index][3]:
            parts[index].append(swapped(piece, "groups", 0))

    def join(m):
        chosen = [i for i, p in enumerate(pieces) if p[0] == m]
        operands = [part for i in chosen for part in parts[i]]
        return pl.pallas_call(
            functools.partial(join_kernel, [pieces[i] for i in chosen]),
            out_shape=jax.ShapeDtypeStruct((width, hid), jnp.bfloat16),
            in_specs=[in_vmem] * len(operands),
            out_specs=in_vmem,
            compiler_params=limited,
        )(*operands)

    columns = jnp.swapaxes(gating_columns[0], 0, 1)
    mask = pl.pallas_call(
        mask_kernel,
        out_shape=jax.ShapeDtypeStruct((8, 128), jnp.int32),
        in_specs=[pl.BlockSpec(memory_space=pltpu.SMEM)] + [in_vmem] * 5,
        out_specs=in_vmem,
        compiler_params=limited,
        name="mask",
    )(expert_choice_grid, *own, rootmean_gain, columns, arriving_microgroups)
    weights = [rootmean_gain, columns, *own, join(0), join(1)]
    own_rows = pending_microgroups[0]
    other_rows = []
    for senders in ((0, places - 1), range(1, places - 1)):
        other_rows.append(lax.ppermute(own_rows, "expert", [(e, places - 1 - e) for e in senders]))
    rows_shape = jax.ShapeDtypeStruct((num_rows, width), jnp.bfloat16)

    def layer(tick, which, inputs, after):
        operands = [mask, *inputs]
        if which == 0:
            operands.append(arriving_microgroups)
        operands += weights
        extras = (which == 0) * ((tick > 0) + (tick + 1 < TICKS))
        return pl.pallas_call(
            functools.partial(layer_kernel, tick, which, TICKS - 1),
            out_shape=[rows_shape] * (1 + extras),
            in_specs=[*[in_vmem] * len(operands), anywhere],
            out_specs=[in_vmem] * (1 + extras),
            compiler_params=pltpu.CompilerParams(vmem_limit_bytes=16 << 20),
        )(*operands, after)

    def ahead(value, flip, wrap):
        last = legs if wrap else legs - 1
        perm = [
            (e * legs + s, (places - 1 - e if flip else e) * legs + (s + 1) % legs)
            for e in range(places)
            for s in range(last)
        ]
        return lax.ppermute(value, ("expert", "section"), perm)

    def back(value):
        return lax.ppermute(value, "section", [((s + 1) % legs, s) for s in range(legs)])

    current = {0: (own_rows,), 1: other_rows}
    outputs = []
    after = own_rows
    for tick in range(TICKS):
        following = {}
        straight = {}
        done = {}
        for which in chunk_order(tick):
            got = layer(tick, which, current[which], after)
            after = done[which] = got[0]
            if tick + 1 < TICKS:
                following[1 - which] = ahead(got[-1], True, True)
                straight[which] = ahead(got[0], False, which == 0)
            elif which == 1:
                mirror = [(e, places - 1 - e) for e in range(places)]
                returned = lax.ppermute(got[0], "expert", mirror)
            if tick and which == 0:
                outputs.append(back(got[1]))
        if tick + 1 < TICKS:
            current = {w: (straight[w], following[w]) for w in (0, 1)}
    return pl.pallas_call(
        gather_kernel,
        out_shape=jax.ShapeDtypeStruct((1, TICKS, num_rows, width), jnp.bfloat16),
        in_specs=[in_vmem] * 4,
        out_specs=anywhere,
        scratch_shapes=[
            pltpu.VMEM((num_rows, width), jnp.bfloat16),
            pltpu.SemaphoreType.DMA((TICKS,)),
        ],
        compiler_params=limited,
        name="gather",
    )(*outputs, done[0], returned)


def chunk_order(tick):
    return (1, 0) if (TICKS - 1 - tick) % 2 == 0 else (0, 1)


def solution(mesh):
    placed = (
        P("section", ("groups", "expert"), None),
        P(None, ("groups", "expert"), None),
        P(None, "section", ("groups", "expert")),
        P("section", None),
        P("section", None, None),
        P("section", "expert", None, None),
        P("section", "expert", None, None),
    )

    paired = mesh.shape["expert"] == 4 and mesh.shape["groups"] == 2

    def per_device(*args):
        if paired and args[4].shape[2] == 2 and args[5].shape[2] % 768 == 0:
            return pairs_per_device(*args)
        return slots_per_device(*args)

    return jax.shard_map(
        per_device,
        mesh=mesh,
        in_specs=placed,
        out_specs=P("section", None, ("groups", "expert"), None),
        check_vma=False,
    )
```
